256 devices in a mesh: pipe: 32 (over y, z), tp: 8 (over x, core).
Axes of the slice: x: 4, y: 4, z: 8, core: 2. Of those that a mesh axis runs over, the one named last changes fastest.
Arguments:
- fwd_resid: bfloat16 [32, 512, 4096], P('pipe', 'tp'), may hold values from -6 to 6
- fwd_query: bfloat16 [32, 512, 4096], P('pipe', None, 'tp'), may hold values from -28 to 28
- fwd_keyval: bfloat16 [32, 2, 512, 1024], P('pipe', None, None, 'tp'), may hold values from -8 to 8
- fwd_micro: int32 [32], P('pipe'), may hold values from 0 to 3
- bwd_query: bfloat16 [32, 512, 4096], P('pipe', None, 'tp'), may hold values from -28 to 28
- bwd_keyval: bfloat16 [32, 2, 512, 1024], P('pipe', None, None, 'tp'), may hold values from -8 to 8
- grad_micro: int32 [32], P('pipe'), may hold values from 0 to 3
- grad_in: bfloat16 [32, 512, 4096], P('pipe', 'tp'), may hold values from -6 to 6
- out_weight: bfloat16 [32, 4096, 4096], P('pipe', 'tp'), may hold values from -0.09375 to 0.09375
- doc_starts: int32 [4, 4], replicated, may hold values from 0 to 511, as said below
Outputs:
- fwd_out: bfloat16 [32, 512, 4096], P('pipe', 'tp')
- grad_query: bfloat16 [32, 512, 4096], P('pipe', None, 'tp')
- grad_keyval: bfloat16 [32, 2, 512, 1024], P('pipe', None, None, 'tp')
- grad_weight: bfloat16 [32, 4096, 4096], P('pipe', 'tp')
The draws below stay inside these ranges and needn't reach their ends.
Inputs may be any that keep to these rules, and one draw needn't show every extreme that they name: `doc_starts`: row m holds the first rows of the 4 documents of micro-batch m: it begins with 0 and rises strictly.
All inputs are finite; a program needn't handle non-finite values.
Results may differ from the reference program's by a relative error of at most 0.007.
Values may be sent and summed in bfloat16 or wider, within the bound.
A program may use at most 128 MiB of HBM per device.

```python
import math
import jax
import jax.numpy as jnp
from jax import lax

R = 512
D = 4096
HEADS = 32
KVH = 8
HD = 128
NDOC = 4
MICRO = 4
PHASES = 32
N_TP = 8


def keys_and_queries(key, which):
    base_key = jax.random.fold_in(key, 7 + which)
    query = jnp.clip(jax.random.normal(jax.random.fold_in(base_key, 1), (PHASES, R, HEADS * HD), jnp.float32), -6.0, 6.0)
    keyval = jnp.clip(jax.random.normal(jax.random.fold_in(base_key, 2), (PHASES, 2, R, KVH * HD), jnp.float32), -6.0, 6.0)
    return (query, keyval)


def draw_fwd_query(key, part):
    return keys_and_queries(key, 0)[0].astype(jnp.bfloat16)


def draw_fwd_keyval(key, part):
    return keys_and_queries(key, 0)[1].astype(jnp.bfloat16)


def draw_bwd_query(key, part):
    return keys_and_queries(key, 1)[0].astype(jnp.bfloat16)


def draw_bwd_keyval(key, part):
    return keys_and_queries(key, 1)[1].astype(jnp.bfloat16)


def draw_doc_starts(key, part):

    def one_row(row_key):
        picked = jax.random.permutation(row_key, R - 1)[:NDOC - 1] + 1
        return jnp.concatenate([jnp.zeros((1,), jnp.int32), jnp.sort(picked).astype(jnp.int32)])
    return jax.vmap(one_row)(jax.random.split(jax.random.fold_in(key, 3), MICRO))


def plant(result, own_key, low, largest):
    spot = [jax.random.randint(jax.random.fold_in(own_key, axis), (), 0, length) for axis, length in enumerate(result.shape)]
    main_axis = result.shape.index(max(result.shape))
    beside = spot[:main_axis] + [(spot[main_axis] + 1) % result.shape[main_axis]] + spot[main_axis + 1:]
    return result.at[tuple(spot)].set(low).at[tuple(beside)].set(largest)


def block_scale(key, extent, pieces, smallest, high):
    level = 1.0
    for dim, blocks in pieces:
        steps = jax.random.uniform(jax.random.fold_in(jax.random.fold_in(key, 6), dim), (blocks,), jnp.float32, smallest / len(pieces), high / len(pieces))
        level = level * jnp.repeat(jnp.exp(steps), extent[dim] // blocks).reshape((-1,) + (1,) * (len(extent) - 1 - dim))
    return level


def gaussian(key, extent, spread, reach, cuts=(), kind=jnp.bfloat16):
    drawn = jax.random.normal(key, extent, jnp.float32) * spread
    if len(cuts) > 0:
        drawn = block_scale(key, extent, cuts, -0.22, 0.18) * drawn
    return jnp.clip(drawn, min=-reach, max=reach).astype(kind)


def setup_inputs(seed: int = 0) -> dict:
    splits = jax.random.split(jax.random.key(seed), 11)
    fwd_resid = gaussian(splits[0], (PHASES, R, D), 1.0, 6.0, ((0, 32), (1, 8)))
    fwd_query = draw_fwd_query(jax.random.fold_in(splits[10], 71), 0)
    fwd_keyval = draw_fwd_keyval(jax.random.fold_in(splits[10], 71), 0)
    fwd_micro = plant(jax.random.randint(splits[3], (PHASES,), 0, MICRO), jax.random.fold_in(splits[3], 1), 0, MICRO - 1).astype(jnp.int32)
    bwd_query = draw_bwd_query(jax.random.fold_in(splits[10], 71), 0)
    bwd_keyval = draw_bwd_keyval(jax.random.fold_in(splits[10], 71), 0)
    grad_micro = plant(jax.random.randint(splits[6], (PHASES,), 0, MICRO), jax.random.fold_in(splits[6], 1), 0, MICRO - 1).astype(jnp.int32)
    grad_in = gaussian(splits[7], (PHASES, R, D), 1.0, 6.0, ((0, 32), (1, 8)))
    out_weight = gaussian(splits[8], (PHASES, HEADS * HD, D), (HEADS * HD) ** -0.5, 0.09375, ((0, 32), (1, 8)))
    doc_starts = draw_doc_starts(jax.random.fold_in(splits[10], 71), 0)
    return dict(fwd_resid=fwd_resid, fwd_query=fwd_query, fwd_keyval=fwd_keyval, fwd_micro=fwd_micro, bwd_query=bwd_query, bwd_keyval=bwd_keyval, grad_micro=grad_micro, grad_in=grad_in, out_weight=out_weight, doc_starts=doc_starts)


def doc_allowed(starts, row_count):
    position = jnp.arange(row_count, dtype=jnp.int32)
    segment = lax.optimization_barrier(jnp.sum((starts[None, :] <= position[:, None]).astype(jnp.int32), axis=1))
    causal = position[None, :] <= position[:, None]
    return causal & (segment[:, None] == segment[None, :])

def pick_starts(start_table, micro_index):
    chosen = jnp.arange(start_table.shape[0], dtype=jnp.int32) == micro_index
    return lax.optimization_barrier(jnp.sum(jnp.where(chosen[:, None], start_table, 0), axis=0)).astype(jnp.int32)

def head_forward(query_head, key_head, value_head, allowed):
    score_scale = 1.0 / math.sqrt(query_head.shape[-1])
    scores = jnp.dot(query_head, key_head.T, preferred_element_type=jnp.float32) * score_scale
    scores = jnp.where(allowed, scores, -1e+30)
    shifted = jnp.exp(scores - lax.optimization_barrier(jnp.max(scores, axis=1, keepdims=True)))
    attn_probs = shifted / lax.optimization_barrier(jnp.sum(shifted, axis=1, keepdims=True))
    output = jnp.dot(attn_probs.astype(jnp.bfloat16), value_head, preferred_element_type=jnp.float32).astype(jnp.bfloat16)
    return (output, attn_probs)

def split_heads(query, keyval):
    row_count = query.shape[0]
    heads_here = query.shape[1] // HD
    groups_here = keyval.shape[2] // HD
    group_size = heads_here // groups_here
    query_heads = query.reshape(row_count, heads_here, HD).transpose(1, 0, 2)
    key_heads = jnp.repeat(keyval[0].reshape(row_count, groups_here, HD).transpose(1, 0, 2), group_size, axis=0)
    value_heads = jnp.repeat(keyval[1].reshape(row_count, groups_here, HD).transpose(1, 0, 2), group_size, axis=0)
    return (query_heads, key_heads, value_heads)

def attend(query, keyval, allowed):
    head_parts = split_heads(query, keyval)
    outputs, attn_probs = jax.vmap(head_forward, in_axes=(0, 0, 0, None))(head_parts[0], head_parts[1], head_parts[2], allowed)
    merged = outputs.transpose(1, 0, 2).reshape(query.shape[0], query.shape[1])
    return (merged, attn_probs, head_parts)

def head_backward(query_head, key_head, value_head, attn_probs, grad_head):
    score_scale = 1.0 / math.sqrt(query_head.shape[-1])
    grad_probs = jnp.dot(grad_head, value_head.T, preferred_element_type=jnp.float32)
    center = lax.optimization_barrier(jnp.sum(attn_probs * grad_probs, axis=1, keepdims=True))
    grad_scores = (attn_probs * (grad_probs - center) * score_scale).astype(jnp.bfloat16)
    grad_query = jnp.dot(grad_scores, key_head, preferred_element_type=jnp.float32).astype(jnp.bfloat16)
    grad_key = jnp.dot(grad_scores.T, query_head, preferred_element_type=jnp.float32)
    grad_value = jnp.dot(attn_probs.astype(jnp.bfloat16).T, grad_head, preferred_element_type=jnp.float32)
    return (grad_query, grad_key, grad_value)

def attend_back(head_parts, attn_probs, grad_attn, keyval):
    query_heads, key_heads, value_heads = head_parts
    heads_here, row_count, head_dim = query_heads.shape
    groups_here = keyval.shape[2] // head_dim
    grad_heads = grad_attn.reshape(row_count, heads_here, head_dim).transpose(1, 0, 2)
    grad_query, grad_key, grad_value = jax.vmap(head_backward)(query_heads, key_heads, value_heads, attn_probs, grad_heads)
    merged_query = grad_query.transpose(1, 0, 2).reshape(row_count, heads_here * head_dim)
    key_sum = grad_key.reshape(groups_here, heads_here // groups_here, row_count, head_dim).sum(axis=1)
    value_sum = grad_value.reshape(groups_here, heads_here // groups_here, row_count, head_dim).sum(axis=1)
    stacked = jnp.stack([key_sum, value_sum]).transpose(0, 2, 1, 3).reshape(2, row_count, groups_here * head_dim)
    return (merged_query, stacked.astype(jnp.bfloat16))

def reference(fwd_resid, fwd_query, fwd_keyval, fwd_micro, bwd_query, bwd_keyval, grad_micro, grad_in, out_weight, doc_starts):
    columns = HEADS * HD // N_TP

    def one_phase(phase_items):
        resid_in, query_in, keyval_in, micro_in, back_query, back_keyval, micro_back, grad_rows, weight = phase_items
        allowed = doc_allowed(pick_starts(doc_starts, micro_in), R)
        attn_out, _, _ = attend(query_in, keyval_in, allowed)
        proj_sum = jnp.zeros((R, D), jnp.float32)
        for block_index in range(N_TP):
            lower = block_index * columns
            partial_sum = jnp.dot(attn_out[:, lower:lower + columns], weight[lower:lower + columns], preferred_element_type=jnp.float32).astype(jnp.bfloat16)
            partial_sum = lax.optimization_barrier(partial_sum)
            proj_sum = proj_sum + partial_sum.astype(jnp.float32)
        phase_out = (resid_in.astype(jnp.float32) + proj_sum).astype(jnp.bfloat16)
        allowed_back = doc_allowed(pick_starts(doc_starts, micro_back), R)
        back_attn, attn_probs, head_parts = attend(back_query, back_keyval, allowed_back)
        grad_attn = jnp.dot(grad_rows, weight.T, preferred_element_type=jnp.float32).astype(jnp.bfloat16)
        weight_grad = jnp.dot(back_attn.T, grad_rows, preferred_element_type=jnp.float32).astype(jnp.bfloat16)
        query_grad, keyval_grad = attend_back(head_parts, attn_probs, grad_attn, back_keyval)
        return (phase_out, query_grad, keyval_grad, weight_grad)
    phase_items = (jnp.roll(fwd_resid, 1, axis=0), jnp.roll(fwd_query, 1, axis=0), jnp.roll(fwd_keyval, 1, axis=0), jnp.roll(fwd_micro, 1, axis=0), bwd_query, bwd_keyval, jnp.roll(grad_micro, -1, axis=0), jnp.roll(grad_in, -1, axis=0), out_weight)
    results = lax.map(one_phase, phase_items)
    return (results[0], results[1], results[2], results[3])
```

```python
import functools
import math

import jax
import jax.numpy as jnp
from jax import lax
from jax.experimental import pallas as pl
from jax.experimental.pallas import tpu as pltpu
from jax.sharding import PartitionSpec as P

MESH = pl.DeviceIdType.MESH
F32 = jnp.float32
BF16 = jnp.bfloat16
R = 512
D = 4096
HD = 128
HALF = D // 2
SCALE = 1.0 / math.sqrt(HD)
EXP_SCALE = SCALE * math.log2(math.e)
MASKED = -1e30
CHUNKS = 4
CROWS = 64 // CHUNKS
TILE = 512
OPP, LEFT, RIGHT, OWN = 0, 1, 2, 3


def dot(a, b):
    return jnp.dot(a, b, preferred_element_type=F32)


def dot_nt(a, b):
    return lax.dot_general(a, b, (((1,), (1,)), ((), ())), preferred_element_type=F32)


def kernel(
    fwd_micro, grad_micro, starts, resid, fq, fkv, bq, bkv, grad, weight,
    out, gq, gkv, gw,
    fq_v, fkv_v, bq_v, bkv_v, w_v, g_v, attn_out, attn_in, resid_in, mic_out, mic_in,
    bias_f, bias_b, kt_v, vt_v, pt_v, bat_v, acc_v, ga_v, dk_v, dv_v, gq_v, gkv_v, gw_v,
    part, recvp, opp_sum, side_sum, rel_l, rel_r, fin_l, fin_r, acc_r, acc_l, out_v,
    ld_sem, st_sem, gw_sem,
    z_s, z_r, mic_s, mic_r, at_s, at_r, rs_s, rs_r,
    xr_s, xl_s, fl_r, fr_r, yr_s, yl_s, fl2_r, fr2_r, p_s, p_r,
    pp_s, pp_r, sr_s, sl_s, sl_r, sr_r,
):
    pipe, tp = lax.axis_index("pipe"), lax.axis_index("tp")
    n_pipe = lax.axis_size("pipe")
    core = lax.rem(tp, 2)
    partner = tp + 1 - 2 * core
    right, left, opp = lax.rem(tp + 2, 8), lax.rem(tp + 6, 8), lax.rem(tp + 4, 8)
    chip = lax.div(tp, 2)
    nxt, prv = lax.rem(pipe + 1, n_pipe), lax.rem(pipe + n_pipe - 1, n_pipe)

    def rcopy(src, dst, send, recv, device):
        return pltpu.make_async_remote_copy(
            src_ref=src, dst_ref=dst, send_sem=send, recv_sem=recv, device_id=device, device_id_type=MESH
        )

    def landed(dst, recv):
        pltpu.make_async_copy(dst, dst, recv).wait()

    loads = [
        pltpu.make_async_copy(src, dst, ld_sem.at[i])
        for i, (src, dst) in enumerate(
            [(fkv, fkv_v), (fq, fq_v), (bkv, bkv_v), (bq, bq_v), (weight, w_v)]
        )
    ]
    for load in loads:
        load.start()
    mic_out[...] = jnp.full(mic_out.shape, grad_micro[0], jnp.int32)

    barrier = pltpu.get_barrier_semaphore()
    peers = ((pipe, partner), (pipe, right), (pipe, left), (nxt, tp), (prv, tp))
    for peer in peers:
        pl.semaphore_signal(barrier, inc=1, device_id=peer, device_id_type=MESH)

    first = [starts[0, d] for d in range(4)]
    for m in range(1, 4):
        first = [jnp.where(fwd_micro[0] == m, starts[m, d], first[d]) for d in range(4)]

    @pl.loop(0, 4)
    def _(block):
        row0 = pl.multiple_of(block * 128, 128)
        row = lax.broadcasted_iota(jnp.int32, (128, R), 0) + row0
        column = lax.broadcasted_iota(jnp.int32, (128, R), 1)
        begin = jnp.zeros((128, R), jnp.int32)
        for d in range(4):
            begin = jnp.maximum(begin, jnp.where(row >= first[d], first[d], 0))
        bias_f[pl.ds(row0, 128), :] = jnp.where((column >= begin) & (column <= row), 0.0, MASKED)

    pl.semaphore_wait(barrier, len(peers))

    def rows_of(shard, k):
        return pl.ds(pl.multiple_of(shard * 64 + k * CROWS, CROWS), CROWS)

    def z_copy(k):
        return rcopy(
            grad.at[pl.ds(pl.multiple_of(k * CROWS, CROWS), CROWS), :], g_v.at[rows_of(tp, k), :],
            z_s.at[k], z_r.at[k], (prv, tp),
        )

    mic = rcopy(mic_out, mic_in, mic_s, mic_r, (prv, tp))
    mic.start()
    for k in range(CHUNKS):
        z_copy(k).start()

    loads[0].wait()
    loads[1].wait()

    def attn_copy(h):
        return rcopy(attn_out.at[h], attn_in.at[h], at_s.at[h], at_r.at[h], (nxt, tp))

    @pl.loop(0, 4)
    def _(h):
        cols = pl.ds(pl.multiple_of(h * HD, HD), HD)
        for b in range(2):
            n = 256 * (b + 1)
            rows = slice(256 * b, n)
            scores = dot_nt(fq_v[rows, cols], fkv_v[0, :n, :]) + bias_f[rows, :n]
            shifted = jnp.exp2((scores - jnp.max(scores, axis=1, keepdims=True)) * EXP_SCALE)
            total = jnp.sum(shifted, axis=1, keepdims=True)
            attn_out[h, rows, :] = (dot(shifted.astype(BF16), fkv_v[1, :n, :]) * (1.0 / total)).astype(BF16)
        attn_copy(h).start()

    resid_copy = rcopy(resid, resid_in, rs_s, rs_r, (nxt, tp))
    resid_copy.start()

    loads[2].wait()
    loads[3].wait()
    mic.wait_recv()
    micro = mic_in[0:1, :]
    begins = []
    for d in range(4):
        value = jnp.zeros((1, 128), jnp.int32)
        for m in range(4):
            value = value + jnp.where(micro == m, starts[m, d], 0)
        begins.append(value)

    @pl.loop(0, 4)
    def _(block):
        col0 = pl.multiple_of(block * 128, 128)
        query = lax.broadcasted_iota(jnp.int32, (1, 128), 1) + col0
        begin = jnp.zeros((1, 128), jnp.int32)
        for d in range(4):
            begin = jnp.maximum(begin, jnp.where(query >= begins[d], begins[d], 0))
        key = lax.broadcasted_iota(jnp.int32, (R, 128), 0)
        bias_b[:, pl.ds(col0, 128)] = jnp.where((key >= begin) & (key <= query), 0.0, MASKED)

    kt_v[...] = bkv_v[0].astype(F32).T.astype(BF16)
    vt_v[...] = bkv_v[1].astype(F32).T.astype(BF16)
    dk_v[...] = jnp.zeros_like(dk_v)
    dv_v[...] = jnp.zeros_like(dv_v)

    half_a, half_b = pl.ds(0, HALF), pl.ds(HALF, HALF)

    def x_copies(k):
        mine = g_v.at[rows_of(tp, k), :]
        return (
            rcopy(mine, mine, xr_s.at[k], fl_r.at[k], (pipe, right)),
            rcopy(mine, mine, xl_s.at[k], fr_r.at[k], (pipe, left)),
            rcopy(mine, mine, p_s.at[0, k], p_r.at[0, k], (pipe, partner)),
        )

    def left_copies(k):
        theirs = g_v.at[rows_of(left, k), half_a]
        whole = g_v.at[rows_of(left, k), :]
        return (
            rcopy(theirs, theirs, yr_s.at[k], fl2_r.at[k], (pipe, right)),
            rcopy(whole, whole, p_s.at[1, k], p_r.at[1, k], (pipe, partner)),
        )

    def right_copies(k):
        theirs = g_v.at[rows_of(right, k), half_b]
        whole = g_v.at[rows_of(right, k), :]
        return (
            rcopy(theirs, theirs, yl_s.at[k], fr2_r.at[k], (pipe, left)),
            rcopy(whole, whole, p_s.at[2, k], p_r.at[2, k], (pipe, partner)),
        )

    def opp_copy(k):
        whole = g_v.at[rows_of(opp, k), :]
        return rcopy(whole, whole, p_s.at[3, k], p_r.at[3, k], (pipe, partner))

    def from_next(k):
        landed(g_v.at[rows_of(tp, k), :], z_r.at[k])
        for copy in x_copies(k):
            copy.start()

    def from_sides(k):
        landed(g_v.at[rows_of(left, k), :], fl_r.at[k])
        for copy in left_copies(k):
            copy.start()
        landed(g_v.at[rows_of(right, k), :], fr_r.at[k])
        for copy in right_copies(k):
            copy.start()

    def from_opp(k):
        landed(g_v.at[rows_of(opp, k), half_a], fl2_r.at[k])
        landed(g_v.at[rows_of(opp, k), half_b], fr2_r.at[k])
        opp_copy(k).start()

    @pl.loop(0, 4)
    def _(k):
        from_next(k)
        cols = pl.ds(pl.multiple_of(k * HD, HD), HD)
        for b in range(2):
            n = 256 * (b + 1)
            rows = slice(256 * b, n)
            scores = dot_nt(bkv_v[0, :n, :], bq_v[rows, cols]) + bias_b[:n, rows]
            shifted = jnp.exp2((scores - jnp.max(scores, axis=0, keepdims=True)) * EXP_SCALE)
            total = jnp.sum(shifted, axis=0, keepdims=True)
            probs = (shifted * (1.0 / total)).astype(BF16)
            pt_v[k, :n, rows] = probs
            bat_v[cols, rows] = dot(vt_v[:, :n], probs).astype(BF16)

        @pl.when(k >= 1)
        def _():
            from_sides(k - 1)

        @pl.when(k >= 2)
        def _():
            from_opp(k - 2)

    loads[4].wait()
    for h in range(4):
        landed(attn_in.at[h], at_r.at[h])
    chip_of = (lax.rem(chip + 2, 4), lax.rem(chip + 3, 4), lax.rem(chip + 1, 4), chip)

    def project(pair, tiles):
        def block(slot):
            rows = pl.ds(pl.multiple_of(chip_of[slot] * 128, 128), 128)
            return jnp.concatenate([attn_in[h, rows, :] for h in range(4)], axis=1)

        lhs = jnp.concatenate([block(slot) for slot in pair], axis=0)

        @pl.loop(tiles[0], tiles[1])
        def _(tile):
            cols = pl.ds(pl.multiple_of(tile * TILE, TILE), TILE)
            product = dot(lhs, w_v[:, cols]).astype(BF16)
            for i, slot in enumerate(pair):
                for c in range(2):
                    part[slot, c, :, cols] = product[128 * i + 64 * c : 128 * i + 64 * c + 64, :]

    halves = (half_a, half_b)

    def pp_copy(slot, half):
        return rcopy(
            part.at[slot, 1 - core, :, halves[half]], recvp.at[slot, :, halves[half]],
            pp_s.at[slot, half], pp_r.at[slot, half], (pipe, partner),
        )

    def chip_sum(slot, half, cols):
        begin = half * HALF + cols
        window = pl.ds(pl.multiple_of(begin, TILE), TILE)
        return part[slot, core, :, window].astype(F32) + recvp[slot, :, window].astype(F32)

    for pair in ((OPP, LEFT), (RIGHT, OWN)):
        for half in range(2):
            project(pair, (4 * half, 4 * half + 4))
            for slot in pair:
                pp_copy(slot, half).start()

    def opp_half(half):
        landed(recvp.at[OPP, :, halves[half]], pp_r.at[OPP, half])

        @pl.loop(0, HALF, step=TILE)
        def _(cols):
            opp_sum[half, :, pl.ds(pl.multiple_of(cols, TILE), TILE)] = chip_sum(OPP, half, cols).astype(BF16)

    send_opp_r = rcopy(opp_sum.at[0], rel_l, sr_s.at[0], sl_r.at[0], (pipe, right))
    send_opp_l = rcopy(opp_sum.at[1], rel_r, sl_s.at[0], sr_r.at[0], (pipe, left))
    send_side_l = rcopy(side_sum.at[0], fin_r.at[0], sl_s.at[1], sr_r.at[1], (pipe, left))
    send_side_r = rcopy(side_sum.at[1], fin_l.at[1], sr_s.at[1], sl_r.at[1], (pipe, right))
    send_acc_r = rcopy(acc_r, fin_l.at[0], sr_s.at[2], sl_r.at[2], (pipe, right))
    send_acc_l = rcopy(acc_l, fin_r.at[1], sl_s.at[2], sr_r.at[2], (pipe, left))

    opp_half(0)
    from_sides(3)
    send_opp_r.start()
    opp_half(1)
    from_opp(2)
    send_opp_l.start()

    def side_half(slot, half):
        landed(recvp.at[slot, :, halves[half]], pp_r.at[slot, half])

        @pl.loop(0, HALF, step=TILE)
        def _(cols):
            side_sum[half, :, pl.ds(pl.multiple_of(cols, TILE), TILE)] = chip_sum(slot, half, cols).astype(BF16)

    side_half(LEFT, 0)
    side_half(RIGHT, 1)
    from_opp(3)
    send_side_l.start()
    send_side_r.start()

    for kind, shard in enumerate((tp + 1 - 2 * core, left + 1 - 2 * core, right + 1 - 2 * core, opp + 1 - 2 * core)):
        for k in range(CHUNKS):
            landed(g_v.at[rows_of(shard, k), :], p_r.at[kind, k])

    acc_v[...] = jnp.zeros_like(acc_v)

    @pl.loop(0, D // TILE)
    def _(tile):
        cols = pl.ds(pl.multiple_of(tile * TILE, TILE), TILE)
        acc_v[...] += dot_nt(g_v[:, cols], w_v[:, cols])

    ga_v[...] = acc_v[...].astype(BF16)

    def gw_copy(tile):
        cols = pl.ds(pl.multiple_of(tile * TILE, TILE), TILE)
        return pltpu.make_async_copy(gw_v.at[:, cols], gw.at[:, cols], gw_sem.at[tile])

    @pl.loop(0, D // TILE)
    def _(tile):
        cols = pl.ds(pl.multiple_of(tile * TILE, TILE), TILE)
        gw_v[:, cols] = dot(bat_v[...], g_v[:, cols]).astype(BF16)
        gw_copy(tile).start()

    landed(rel_l, sl_r.at[0])
    landed(recvp.at[RIGHT, :, half_a], pp_r.at[RIGHT, 0])
    landed(rel_r, sr_r.at[0])
    landed(recvp.at[LEFT, :, half_b], pp_r.at[LEFT, 1])

    @pl.loop(0, HALF, step=TILE)
    def _(cols):
        window = pl.ds(pl.multiple_of(cols, TILE), TILE)
        acc_r[:, window] = (chip_sum(RIGHT, 0, cols) + rel_l[:, window].astype(F32)).astype(BF16)
        acc_l[:, window] = (chip_sum(LEFT, 1, cols) + rel_r[:, window].astype(F32)).astype(BF16)

    send_acc_r.start()
    send_acc_l.start()

    @pl.loop(0, 4)
    def _(h):
        cols = pl.ds(pl.multiple_of(h * HD, HD), HD)
        for b in range(2):
            n = 256 * (b + 1)
            rows = slice(256 * b, n)
            grad_rows = ga_v[rows, cols]
            dprob = dot_nt(bkv_v[1, :n, :], grad_rows)
            probs = pt_v[h, :n, rows]
            wide = probs.astype(F32)
            delta = jnp.sum(wide * dprob, axis=0, keepdims=True)
            dscore = (wide * (dprob - delta) * SCALE).astype(BF16)
            gq_v[rows, cols] = dot(kt_v[:, :n], dscore).T.astype(BF16)
            dk_v[:n, :] += dot(dscore, bq_v[rows, cols])
            dv_v[:n, :] += dot(probs, grad_rows)

    gkv_v[0] = dk_v[...].astype(BF16)
    gkv_v[1] = dv_v[...].astype(BF16)
    stores = [pltpu.make_async_copy(gq_v, gq, st_sem.at[0]), pltpu.make_async_copy(gkv_v, gkv, st_sem.at[1])]
    for store in stores:
        store.start()

    resid_copy.wait_recv()
    for half in range(2):
        landed(recvp.at[OWN, :, halves[half]], pp_r.at[OWN, half])
        landed(fin_l.at[half], sl_r.at[2 if half == 0 else 1])
        landed(fin_r.at[half], sr_r.at[1 if half == 0 else 2])

        @pl.loop(0, HALF, step=TILE)
        def _(cols):
            window = pl.ds(pl.multiple_of(cols, TILE), TILE)
            place = pl.ds(pl.multiple_of(half * HALF + cols, TILE), TILE)
            total = chip_sum(OWN, half, cols) + fin_l[half, :, window].astype(F32) + fin_r[half, :, window].astype(F32)
            out_v[:, place] = (resid_in[:, place].astype(F32) + total).astype(BF16)

        store = pltpu.make_async_copy(out_v.at[:, halves[half]], out.at[:, halves[half]], st_sem.at[2 + half])
        store.start()
        stores.append(store)

    mic.wait_send()
    resid_copy.wait_send()
    for h in range(4):
        attn_copy(h).wait_send()
    for k in range(CHUNKS):
        z_copy(k).wait_send()
        for copy in (*x_copies(k), *left_copies(k), *right_copies(k), opp_copy(k)):
            copy.wait_send()
    for slot in range(4):
        for half in range(2):
            pp_copy(slot, half).wait_send()
    for copy in (send_opp_r, send_opp_l, send_side_l, send_side_r, send_acc_r, send_acc_l):
        copy.wait_send()
    for tile in range(D // TILE):
        gw_copy(tile).wait()
    for store in stores:
        store.wait()


def shards(fwd_resid, fwd_query, fwd_keyval, fwd_micro, bwd_query, bwd_keyval, grad_micro, grad_in, out_weight, doc_starts):
    any_space = pl.BlockSpec(memory_space=pl.ANY)
    smem = pl.BlockSpec(memory_space=pltpu.SMEM)
    dma = pltpu.SemaphoreType.DMA
    vmem = pltpu.VMEM
    scratch = [
        vmem((R, R), BF16), vmem((2, R, HD), BF16), vmem((R, R), BF16), vmem((2, R, HD), BF16),
        vmem((R, D), BF16), vmem((R, D), BF16),
        vmem((4, R, HD), BF16), vmem((4, R, HD), BF16), vmem((64, D), BF16),
        vmem((8, 128), jnp.int32), vmem((8, 128), jnp.int32),
        vmem((R, R), F32), vmem((R, R), F32), vmem((HD, R), BF16), vmem((HD, R), BF16),
        vmem((4, R, R), BF16), vmem((R, R), BF16), vmem((R, R), F32), vmem((R, R), BF16),
        vmem((R, HD), F32), vmem((R, HD), F32), vmem((R, R), BF16), vmem((2, R, HD), BF16), vmem((R, D), BF16),
        vmem((4, 2, 64, D), BF16), vmem((4, 64, D), BF16), vmem((2, 64, HALF), BF16), vmem((2, 64, HALF), BF16),
        vmem((64, HALF), BF16), vmem((64, HALF), BF16), vmem((2, 64, HALF), BF16), vmem((2, 64, HALF), BF16),
        vmem((64, HALF), BF16), vmem((64, HALF), BF16), vmem((64, D), BF16),
        dma((5,)), dma((4,)), dma((D // TILE,)),
        dma((CHUNKS,)), dma((CHUNKS,)), dma, dma, dma((4,)), dma((4,)), dma, dma,
        dma((CHUNKS,)), dma((CHUNKS,)), dma((CHUNKS,)), dma((CHUNKS,)),
        dma((CHUNKS,)), dma((CHUNKS,)), dma((CHUNKS,)), dma((CHUNKS,)),
        dma((4, CHUNKS)), dma((4, CHUNKS)),
        dma((4, 2)), dma((4, 2)), dma((3,)), dma((3,)), dma((3,)), dma((3,)),
    ]
    out, gq, gkv, gw = pl.pallas_call(
        kernel,
        out_shape=(
            jax.ShapeDtypeStruct((64, D), BF16),
            jax.ShapeDtypeStruct((R, R), BF16),
            jax.ShapeDtypeStruct((2, R, HD), BF16),
            jax.ShapeDtypeStruct((R, D), BF16),
        ),
        in_specs=[smem] * 3 + [any_space] * 7,
        out_specs=(any_space,) * 4,
        scratch_shapes=scratch,
        compiler_params=pltpu.CompilerParams(
            collective_id=0, has_side_effects=True, vmem_limit_bytes=60 * 1024 * 1024
        ),
    )(
        fwd_micro, grad_micro, doc_starts, fwd_resid[0], fwd_query[0], fwd_keyval[0],
        bwd_query[0], bwd_keyval[0], grad_in[0], out_weight[0],
    )
    return (out[None], gq[None], gkv[None], gw[None])


def solution(mesh):
    return jax.shard_map(
        shards,
        mesh=mesh,
        in_specs=(
            P("pipe", "tp", None),
            P("pipe", None, "tp"),
            P("pipe", None, None, "tp"),
            P("pipe"),
            P("pipe", None, "tp"),
            P("pipe", None, None, "tp"),
            P("pipe"),
            P("pipe", "tp", None),
            P("pipe", "tp", None),
            P(),
        ),
        out_specs=(
            P("pipe", "tp", None),
            P("pipe", None, "tp"),
            P("pipe", None, None, "tp"),
            P("pipe", "tp", None),
        ),
        check_vma=False,
    )
```

```python
import functools
import math

import jax
import jax.numpy as jnp
from jax import lax
from jax.experimental import pallas as pl
from jax.experimental.pallas import tpu as pltpu
from jax.sharding import PartitionSpec as P

MESH = pl.DeviceIdType.MESH
F32 = jnp.float32
BF16 = jnp.bfloat16
R = 512
D = 4096
HD = 128
HALF = D // 2
SCALE = 1.0 / math.sqrt(HD)
EXP_SCALE = SCALE * math.log2(math.e)
MASKED = -1e30
CHUNKS = 4
CROWS = 64 // CHUNKS
TILE = 512
OPP, LEFT, RIGHT, OWN = 0, 1, 2, 3


def dot(a, b):
    return jnp.dot(a, b, preferred_element_type=F32)


def dot_nt(a, b):
    return lax.dot_general(a, b, (((1,), (1,)), ((), ())), preferred_element_type=F32)


def kernel(
    fwd_micro, grad_micro, starts, resid, fq, fkv, bq, bkv, grad, weight,
    out, gq, gkv, gw,
    fq_v, fkv_v, bq_v, bkv_v, w_v, g_v, attn_out, attn_in, resid_in, mic_out, mic_in,
    bias_f, bias_b, kt_v, vt_v, pt_v, bat_v, acc_v, ga_v, dk_v, dv_v, gq_v, gkv_v, gw_v,
    part, recvp, opp_sum, side_sum, rel_l, rel_r, fin_l, fin_r, acc_r, acc_l, out_v,
    ld_sem, st_sem, gw_sem,
    z_s, z_r, mic_s, mic_r, at_s, at_r, rs_s, rs_r,
    xr_s, xl_s, fl_r, fr_r, yr_s, yl_s, fl2_r, fr2_r, p_s, p_r,
    pp_s, pp_r, sr_s, sl_s, sl_r, sr_r,
):
    pipe, tp = lax.axis_index("pipe"), lax.axis_index("tp")
    n_pipe = lax.axis_size("pipe")
    core = lax.rem(tp, 2)
    partner = tp + 1 - 2 * core
    right, left, opp = lax.rem(tp + 2, 8), lax.rem(tp + 6, 8), lax.rem(tp + 4, 8)
    chip = lax.div(tp, 2)
    nxt, prv = lax.rem(pipe + 1, n_pipe), lax.rem(pipe + n_pipe - 1, n_pipe)

    def rcopy(src, dst, send, recv, device):
        return pltpu.make_async_remote_copy(
            src_ref=src, dst_ref=dst, send_sem=send, recv_sem=recv, device_id=device, device_id_type=MESH
        )

    def landed(dst, recv):
        pltpu.make_async_copy(dst, dst, recv).wait()

    loads = [
        pltpu.make_async_copy(src, dst, ld_sem.at[i])
        for i, (src, dst) in enumerate(
            [(fkv, fkv_v), (fq, fq_v), (bkv, bkv_v), (bq, bq_v), (weight, w_v)]
        )
    ]
    for load in loads:
        load.start()
    mic_out[...] = jnp.full(mic_out.shape, grad_micro[0], jnp.int32)

    barrier = pltpu.get_barrier_semaphore()
    peers = ((pipe, partner), (pipe, right), (pipe, left), (nxt, tp), (prv, tp))
    for peer in peers:
        pl.semaphore_signal(barrier, inc=1, device_id=peer, device_id_type=MESH)

    first = [starts[0, d] for d in range(4)]
    for m in range(1, 4):
        first = [jnp.where(fwd_micro[0] == m, starts[m, d], first[d]) for d in range(4)]

    @pl.loop(0, 4)
    def _(block):
        row0 = pl.multiple_of(block * 128, 128)
        row = lax.broadcasted_iota(jnp.int32, (128, R), 0) + row0
        column = lax.broadcasted_iota(jnp.int32, (128, R), 1)
        begin = jnp.zeros((128, R), jnp.int32)
        for d in range(4):
            begin = jnp.maximum(begin, jnp.where(row >= first[d], first[d], 0))
        bias_f[pl.ds(row0, 128), :] = jnp.where((column >= begin) & (column <= row), 0.0, MASKED)

    pl.semaphore_wait(barrier, len(peers))

    def rows_of(shard, k):
        return pl.ds(pl.multiple_of(shard * 64 + k * CROWS, CROWS), CROWS)

    def z_copy(k):
        return rcopy(
            grad.at[pl.ds(pl.multiple_of(k * CROWS, CROWS), CROWS), :], g_v.at[rows_of(tp, k), :],
            z_s.at[k], z_r.at[k], (prv, tp),
        )

    mic = rcopy(mic_out, mic_in, mic_s, mic_r, (prv, tp))
    mic.start()
    for k in range(CHUNKS):
        z_copy(k).start()

    loads[0].wait()
    loads[1].wait()

    def attn_copy(h):
        return rcopy(attn_out.at[h], attn_in.at[h], at_s.at[h], at_r.at[h], (nxt, tp))

    @pl.loop(0, 4)
    def _(h):
        cols = pl.ds(pl.multiple_of(h * HD, HD), HD)
        for b in range(2):
            n = 256 * (b + 1)
            rows = slice(256 * b, n)
            scores = dot_nt(fq_v[rows, cols], fkv_v[0, :n, :]) + bias_f[rows, :n]
            shifted = jnp.exp2((scores - jnp.max(scores, axis=1, keepdims=True)) * EXP_SCALE)
            total = jnp.sum(shifted, axis=1, keepdims=True)
            attn_out[h, rows, :] = (dot(shifted.astype(BF16), fkv_v[1, :n, :]) * (1.0 / total)).astype(BF16)
        attn_copy(h).start()

    resid_copy = rcopy(resid, resid_in, rs_s, rs_r, (nxt, tp))
    resid_copy.start()

    loads[2].wait()
    loads[3].wait()
    mic.wait_recv()
    micro = mic_in[0:1, :]
    begins = []
    for d in range(4):
        value = jnp.zeros((1, 128), jnp.int32)
        for m in range(4):
            value = value + jnp.where(micro == m, starts[m, d], 0)
        begins.append(value)

    @pl.loop(0, 4)
    def _(block):
        col0 = pl.multiple_of(block * 128, 128)
        query = lax.broadcasted_iota(jnp.int32, (1, 128), 1) + col0
        begin = jnp.zeros((1, 128), jnp.int32)
        for d in range(4):
            begin = jnp.maximum(begin, jnp.where(query >= begins[d], begins[d], 0))
        key = lax.broadcasted_iota(jnp.int32, (R, 128), 0)
        bias_b[:, pl.ds(col0, 128)] = jnp.where((key >= begin) & (key <= query), 0.0, MASKED)

    kt_v[...] = bkv_v[0].astype(F32).T.astype(BF16)
    vt_v[...] = bkv_v[1].astype(F32).T.astype(BF16)
    dk_v[...] = jnp.zeros_like(dk_v)
    dv_v[...] = jnp.zeros_like(dv_v)

    half_a, half_b = pl.ds(0, HALF), pl.ds(HALF, HALF)

    def x_copies(k):
        mine = g_v.at[rows_of(tp, k), :]
        return (
            rcopy(mine, mine, xr_s.at[k], fl_r.at[k], (pipe, right)),
            rcopy(mine, mine, xl_s.at[k], fr_r.at[k], (pipe, left)),
            rcopy(mine, mine, p_s.at[0, k], p_r.at[0, k], (pipe, partner)),
        )

    def left_copies(k):
        theirs = g_v.at[rows_of(left, k), half_a]
        whole = g_v.at[rows_of(left, k), :]
        return (
            rcopy(theirs, theirs, yr_s.at[k], fl2_r.at[k], (pipe, right)),
            rcopy(whole, whole, p_s.at[1, k], p_r.at[1, k], (pipe, partner)),
        )

    def right_copies(k):
        theirs = g_v.at[rows_of(right, k), half_b]
        whole = g_v.at[rows_of(right, k), :]
        return (
            rcopy(theirs, theirs, yl_s.at[k], fr2_r.at[k], (pipe, left)),
            rcopy(whole, whole, p_s.at[2, k], p_r.at[2, k], (pipe, partner)),
        )

    def opp_copy(k):
        whole = g_v.at[rows_of(opp, k), :]
        return rcopy(whole, whole, p_s.at[3, k], p_r.at[3, k], (pipe, partner))

    def from_next(k):
        landed(g_v.at[rows_of(tp, k), :], z_r.at[k])
        for copy in x_copies(k):
            copy.start()

    def from_sides(k):
        landed(g_v.at[rows_of(left, k), :], fl_r.at[k])
        for copy in left_copies(k):
            copy.start()
        landed(g_v.at[rows_of(right, k), :], fr_r.at[k])
        for copy in right_copies(k):
            copy.start()

    def from_opp(k):
        landed(g_v.at[rows_of(opp, k), half_a], fl2_r.at[k])
        landed(g_v.at[rows_of(opp, k), half_b], fr2_r.at[k])
        opp_copy(k).start()

    @pl.loop(0, 4)
    def _(h):
        @pl.when(h == 3)
        def _():
            from_next(0)

        cols = pl.ds(pl.multiple_of(h * HD, HD), HD)
        for b in range(2):
            n = 256 * (b + 1)
            rows = slice(256 * b, n)
            scores = dot_nt(bkv_v[0, :n, :], bq_v[rows, cols]) + bias_b[:n, rows]
            shifted = jnp.exp2((scores - jnp.max(scores, axis=0, keepdims=True)) * EXP_SCALE)
            total = jnp.sum(shifted, axis=0, keepdims=True)
            probs = (shifted * (1.0 / total)).astype(BF16)
            pt_v[h, :n, rows] = probs
            bat_v[cols, rows] = dot(vt_v[:, :n], probs).astype(BF16)

    from_next(1)
    from_sides(0)
    from_next(2)
    from_sides(1)
    from_opp(0)
    from_next(3)

    loads[4].wait()
    for h in range(4):
        landed(attn_in.at[h], at_r.at[h])
    chip_of = (lax.rem(chip + 2, 4), lax.rem(chip + 3, 4), lax.rem(chip + 1, 4), chip)

    def project(pair, tiles):
        def block(slot):
            rows = pl.ds(pl.multiple_of(chip_of[slot] * 128, 128), 128)
            return jnp.concatenate([attn_in[h, rows, :] for h in range(4)], axis=1)

        lhs = jnp.concatenate([block(slot) for slot in pair], axis=0)

        @pl.loop(tiles[0], tiles[1])
        def _(tile):
            cols = pl.ds(pl.multiple_of(tile * TILE, TILE), TILE)
            product = dot(lhs, w_v[:, cols]).astype(BF16)
            for i, slot in enumerate(pair):
                for c in range(2):
                    part[slot, c, :, cols] = product[128 * i + 64 * c : 128 * i + 64 * c + 64, :]

    halves = (half_a, half_b)

    def pp_copy(slot, half):
        return rcopy(
            part.at[slot, 1 - core, :, halves[half]], recvp.at[slot, :, halves[half]],
            pp_s.at[slot, half], pp_r.at[slot, half], (pipe, partner),
        )

    def chip_sum(slot, half, cols):
        begin = half * HALF + cols
        window = pl.ds(pl.multiple_of(begin, TILE), TILE)
        return part[slot, core, :, window].astype(F32) + recvp[slot, :, window].astype(F32)

    def project_pair(pair):
        for half in range(2):
            project(pair, (4 * half, 4 * half + 4))
            for slot in pair:
                pp_copy(slot, half).start()

    project_pair((OPP, LEFT))
    from_sides(2)
    project_pair((RIGHT, OWN))
    from_opp(1)

    def opp_half(half):
        landed(recvp.at[OPP, :, halves[half]], pp_r.at[OPP, half])

        @pl.loop(0, HALF, step=TILE)
        def _(cols):
            opp_sum[half, :, pl.ds(pl.multiple_of(cols, TILE), TILE)] = chip_sum(OPP, half, cols).astype(BF16)

    send_opp_r = rcopy(opp_sum.at[0], rel_l, sr_s.at[0], sl_r.at[0], (pipe, right))
    send_opp_l = rcopy(opp_sum.at[1], rel_r, sl_s.at[0], sr_r.at[0], (pipe, left))
    send_side_l = rcopy(side_sum.at[0], fin_r.at[0], sl_s.at[1], sr_r.at[1], (pipe, left))
    send_side_r = rcopy(side_sum.at[1], fin_l.at[1], sr_s.at[1], sl_r.at[1], (pipe, right))
    send_acc_r = rcopy(acc_r, fin_l.at[0], sr_s.at[2], sl_r.at[2], (pipe, right))
    send_acc_l = rcopy(acc_l, fin_r.at[1], sl_s.at[2], sr_r.at[2], (pipe, left))

    opp_half(0)
    opp_half(1)
    from_sides(3)
    send_opp_r.start()
    send_opp_l.start()

    def side_half(slot, half):
        landed(recvp.at[slot, :, halves[half]], pp_r.at[slot, half])

        @pl.loop(0, HALF, step=TILE)
        def _(cols):
            side_sum[half, :, pl.ds(pl.multiple_of(cols, TILE), TILE)] = chip_sum(slot, half, cols).astype(BF16)

    side_half(LEFT, 0)
    side_half(RIGHT, 1)
    send_side_l.start()
    send_side_r.start()

    peer_shards = [lax.rem(shard, 8) + 1 - 2 * core for shard in (tp, left, right, opp)]

    def attn_grad(half):
        for k in (2 * half, 2 * half + 1):
            for kind, shard in enumerate(peer_shards):
                landed(g_v.at[rows_of(shard, k), :], p_r.at[kind, k])
        acc_v[...] = jnp.zeros_like(acc_v)

        @pl.loop(0, D // TILE)
        def _(tile):
            cols = pl.ds(pl.multiple_of(tile * TILE, TILE), TILE)
            lhs = jnp.concatenate([g_v[64 * i + 32 * half : 64 * i + 32 * half + 32, cols] for i in range(8)], axis=0)
            acc_v[...] += dot_nt(lhs, w_v[:, cols])

        for i in range(8):
            ga_v[64 * i + 32 * half : 64 * i + 32 * half + 32, :] = acc_v[32 * i : 32 * i + 32, :].astype(BF16)

    attn_grad(0)
    from_opp(2)
    from_opp(3)
    attn_grad(1)

    def gw_copy(tile):
        cols = pl.ds(pl.multiple_of(tile * TILE, TILE), TILE)
        return pltpu.make_async_copy(gw_v.at[:, cols], gw.at[:, cols], gw_sem.at[tile])

    @pl.loop(0, D // TILE)
    def _(tile):
        cols = pl.ds(pl.multiple_of(tile * TILE, TILE), TILE)
        gw_v[:, cols] = dot(bat_v[...], g_v[:, cols]).astype(BF16)
        gw_copy(tile).start()

    landed(rel_l, sl_r.at[0])
    landed(recvp.at[RIGHT, :, half_a], pp_r.at[RIGHT, 0])
    landed(rel_r, sr_r.at[0])
    landed(recvp.at[LEFT, :, half_b], pp_r.at[LEFT, 1])

    @pl.loop(0, HALF, step=TILE)
    def _(cols):
        window = pl.ds(pl.multiple_of(cols, TILE), TILE)
        acc_r[:, window] = (chip_sum(RIGHT, 0, cols) + rel_l[:, window].astype(F32)).astype(BF16)
        acc_l[:, window] = (chip_sum(LEFT, 1, cols) + rel_r[:, window].astype(F32)).astype(BF16)

    send_acc_r.start()
    send_acc_l.start()

    @pl.loop(0, 4)
    def _(h):
        cols = pl.ds(pl.multiple_of(h * HD, HD), HD)
        for b in range(2):
            n = 256 * (b + 1)
            rows = slice(256 * b, n)
            grad_rows = ga_v[rows, cols]
            dprob = dot_nt(bkv_v[1, :n, :], grad_rows)
            probs = pt_v[h, :n, rows]
            wide = probs.astype(F32)
            delta = jnp.sum(wide * dprob, axis=0, keepdims=True)
            dscore = (wide * (dprob - delta) * SCALE).astype(BF16)
            gq_v[rows, cols] = dot(kt_v[:, :n], dscore).T.astype(BF16)
            dk_v[:n, :] += dot(dscore, bq_v[rows, cols])
            dv_v[:n, :] += dot(probs, grad_rows)

    gkv_v[0] = dk_v[...].astype(BF16)
    gkv_v[1] = dv_v[...].astype(BF16)
    stores = [pltpu.make_async_copy(gq_v, gq, st_sem.at[0]), pltpu.make_async_copy(gkv_v, gkv, st_sem.at[1])]
    for store in stores:
        store.start()

    resid_copy.wait_recv()
    for half in range(2):
        landed(recvp.at[OWN, :, halves[half]], pp_r.at[OWN, half])
        landed(fin_l.at[half], sl_r.at[2 if half == 0 else 1])
        landed(fin_r.at[half], sr_r.at[1 if half == 0 else 2])

        @pl.loop(0, HALF, step=TILE)
        def _(cols):
            window = pl.ds(pl.multiple_of(cols, TILE), TILE)
            place = pl.ds(pl.multiple_of(half * HALF + cols, TILE), TILE)
            total = chip_sum(OWN, half, cols) + fin_l[half, :, window].astype(F32) + fin_r[half, :, window].astype(F32)
            out_v[:, place] = (resid_in[:, place].astype(F32) + total).astype(BF16)

        store = pltpu.make_async_copy(out_v.at[:, halves[half]], out.at[:, halves[half]], st_sem.at[2 + half])
        store.start()
        stores.append(store)

    mic.wait_send()
    resid_copy.wait_send()
    for h in range(4):
        attn_copy(h).wait_send()
    for k in range(CHUNKS):
        z_copy(k).wait_send()
        for copy in (*x_copies(k), *left_copies(k), *right_copies(k), opp_copy(k)):
            copy.wait_send()
    for slot in range(4):
        for half in range(2):
            pp_copy(slot, half).wait_send()
    for copy in (send_opp_r, send_opp_l, send_side_l, send_side_r, send_acc_r, send_acc_l):
        copy.wait_send()
    for tile in range(D // TILE):
        gw_copy(tile).wait()
    for store in stores:
        store.wait()


def deliver(*refs):
    srcs, dsts, sem = refs[:4], refs[4:8], refs[8]
    pieces = []
    for src, dst in zip(srcs, dsts):
        rows = src.shape[-2]
        for lead in range(src.shape[0]):
            for row in range(0, rows, 64):
                pieces.append(tuple(ref.at[lead, pl.ds(row, 64), :] for ref in (src, dst)))
    copies = [pltpu.make_async_copy(a, b, sem.at[i]) for i, (a, b) in enumerate(pieces)]
    for copy in copies:
        copy.start()
    for copy in copies:
        copy.wait()


def shards(fwd_resid, fwd_query, fwd_keyval, fwd_micro, bwd_query, bwd_keyval, grad_micro, grad_in, out_weight, doc_starts):
    any_space = pl.BlockSpec(memory_space=pl.ANY)
    smem = pl.BlockSpec(memory_space=pltpu.SMEM)
    dma = pltpu.SemaphoreType.DMA
    vmem = pltpu.VMEM
    scratch = [
        vmem((R, R), BF16), vmem((2, R, HD), BF16), vmem((R, R), BF16), vmem((2, R, HD), BF16),
        vmem((R, D), BF16), vmem((R, D), BF16),
        vmem((4, R, HD), BF16), vmem((4, R, HD), BF16), vmem((64, D), BF16),
        vmem((8, 128), jnp.int32), vmem((8, 128), jnp.int32),
        vmem((R, R), F32), vmem((R, R), F32), vmem((HD, R), BF16), vmem((HD, R), BF16),
        vmem((4, R, R), BF16), vmem((R, R), BF16), vmem((R // 2, R), F32), vmem((R, R), BF16),
        vmem((R, HD), F32), vmem((R, HD), F32), vmem((R, R), BF16), vmem((2, R, HD), BF16), vmem((R, D), BF16),
        vmem((4, 2, 64, D), BF16), vmem((4, 64, D), BF16), vmem((2, 64, HALF), BF16), vmem((2, 64, HALF), BF16),
        vmem((64, HALF), BF16), vmem((64, HALF), BF16), vmem((2, 64, HALF), BF16), vmem((2, 64, HALF), BF16),
        vmem((64, HALF), BF16), vmem((64, HALF), BF16), vmem((64, D), BF16),
        dma((5,)), dma((4,)), dma((D // TILE,)),
        dma((CHUNKS,)), dma((CHUNKS,)), dma, dma, dma((4,)), dma((4,)), dma, dma,
        dma((CHUNKS,)), dma((CHUNKS,)), dma((CHUNKS,)), dma((CHUNKS,)),
        dma((CHUNKS,)), dma((CHUNKS,)), dma((CHUNKS,)), dma((CHUNKS,)),
        dma((4, CHUNKS)), dma((4, CHUNKS)),
        dma((4, 2)), dma((4, 2)), dma((3,)), dma((3,)), dma((3,)), dma((3,)),
    ]
    out, gq, gkv, gw = pl.pallas_call(
        kernel,
        out_shape=(
            jax.ShapeDtypeStruct((64, D), BF16),
            jax.ShapeDtypeStruct((R, R), BF16),
            jax.ShapeDtypeStruct((2, R, HD), BF16),
            jax.ShapeDtypeStruct((R, D), BF16),
        ),
        in_specs=[smem] * 3 + [pl.BlockSpec(memory_space=pltpu.HBM)] * 7,
        out_specs=(any_space,) * 4,
        scratch_shapes=scratch,
        compiler_params=pltpu.CompilerParams(
            collective_id=0, has_side_effects=True, vmem_limit_bytes=40 * 1024 * 1024
        ),
    )(
        fwd_micro, grad_micro, pltpu.with_memory_space_constraint(doc_starts, pltpu.HBM),
        *(
            pltpu.with_memory_space_constraint(a[0], pltpu.HBM)
            for a in (fwd_resid, fwd_query, fwd_keyval, bwd_query, bwd_keyval, grad_in, out_weight)
        ),
    )
    arrays = (gw[None], gq[None], gkv, out[None])
    count = sum(a.shape[0] * max(a.shape[1] // 64, 1) for a in arrays)
    gw, gq, gkv, out = pl.pallas_call(
        deliver,
        out_shape=tuple(jax.ShapeDtypeStruct(a.shape, a.dtype) for a in arrays),
        in_specs=[any_space] * 4,
        out_specs=(any_space,) * 4,
        scratch_shapes=[dma((count,))],
        compiler_params=pltpu.CompilerParams(vmem_limit_bytes=4 * 1024 * 1024),
    )(*arrays)
    return (out, gq, gkv[None], gw)


def solution(mesh):
    return jax.shard_map(
        shards,
        mesh=mesh,
        in_specs=(
            P("pipe", "tp", None),
            P("pipe", None, "tp"),
            P("pipe", None, None, "tp"),
            P("pipe"),
            P("pipe", None, "tp"),
            P("pipe", None, None, "tp"),
            P("pipe"),
            P("pipe", "tp", None),
            P("pipe", "tp", None),
            P(),
        ),
        out_specs=(
            P("pipe", "tp", None),
            P("pipe", None, "tp"),
            P("pipe", None, None, "tp"),
            P("pipe", "tp", None),
        ),
        check_vma=False,
    )
```

```python
import functools
import math

import jax
import jax.numpy as jnp
from jax import lax
from jax.experimental import pallas as pl
from jax.experimental.pallas import tpu as pltpu
from jax.sharding import PartitionSpec as P

MESH = pl.DeviceIdType.MESH
F32 = jnp.float32
BF16 = jnp.bfloat16
R = 512
D = 4096
HD = 128
HALF = D // 2
SCALE = 1.0 / math.sqrt(HD)
EXP_SCALE = SCALE * math.log2(math.e)
MASKED = -1e30
CHUNKS = 4
CROWS = 64 // CHUNKS
TILE = 512
DEEP = 1024
PIECES = ((0, 0, HALF), (0, HALF, HALF), (1, 0, D), (2, 0, D), (3, 0, D))
LAST = len(PIECES) - 1
OPP, LEFT, OWN, RIGHT = 0, 1, 2, 3


def dot(a, b):
    return jnp.dot(a, b, preferred_element_type=F32)


def dot_nt(a, b):
    return lax.dot_general(a, b, (((1,), (1,)), ((), ())), preferred_element_type=F32)


def kernel(
    fwd_micro, grad_micro, starts, resid, fq, fkv, bq, bkv, grad, weight,
    out, gq, gkv, gw,
    fq_v, fkv_v, bq_v, bkv_v, w_v, g_v, attn_out, attn_in, resid_in, mic_out, mic_in,
    bias_b, kt_v, vt_v, pt_v, bat_v, acc_v, ga_v, dk_v, dv_v, gq_v, gkv_v, gw_v,
    part, recvp, opp_sum, side_sum, rel_l, rel_r, fin_l, fin_r, acc_r, acc_l, out_v,
    ld_sem, st_sem, gw_sem,
    early_l, early_r, el_s, el_r, er_s, er_r, ez_s, ez_r,
    z_s, z_r, mic_s, mic_r, at_s, at_r, rs_s, rs_r,
    xr_s, xl_s, fl_r, fr_r, yr_s, yl_s, fl2_r, fr2_r, p_s, p_r,
    pp_s, pp_r, sr_s, sl_s, sl_r, sr_r,
):
    pipe, tp = lax.axis_index("pipe"), lax.axis_index("tp")
    n_pipe = lax.axis_size("pipe")
    core = lax.rem(tp, 2)
    partner = tp + 1 - 2 * core
    right, left, opp = lax.rem(tp + 2, 8), lax.rem(tp + 6, 8), lax.rem(tp + 4, 8)
    chip = lax.div(tp, 2)
    nxt, prv = lax.rem(pipe + 1, n_pipe), lax.rem(pipe + n_pipe - 1, n_pipe)

    def rcopy(src, dst, send, recv, device):
        return pltpu.make_async_remote_copy(
            src_ref=src, dst_ref=dst, send_sem=send, recv_sem=recv, device_id=device, device_id_type=MESH
        )

    def landed(dst, recv):
        pltpu.make_async_copy(dst, dst, recv).wait()

    loads = [
        pltpu.make_async_copy(src, dst, ld_sem.at[i])
        for i, (src, dst) in enumerate(
            [(fkv, fkv_v), (fq, fq_v), (bkv, bkv_v), (bq, bq_v), (weight, w_v)]
        )
    ]
    for load in loads:
        load.start()
    mic_out[...] = jnp.full(mic_out.shape, grad_micro[0], jnp.int32)

    barrier = pltpu.get_barrier_semaphore()
    peers = ((pipe, partner), (pipe, right), (pipe, left), (nxt, tp), (prv, tp))
    for peer in peers:
        pl.semaphore_signal(barrier, inc=1, device_id=peer, device_id_type=MESH)

    first = [starts[0, d] for d in range(4)]
    for m in range(1, 4):
        first = [jnp.where(fwd_micro[0] == m, starts[m, d], first[d]) for d in range(4)]

    pl.semaphore_wait(barrier, len(peers))

    def rows_of(shard, k):
        return pl.ds(pl.multiple_of(shard * 64 + k * CROWS, CROWS), CROWS)

    def view(shard, p):
        chunk, first_col, cols = PIECES[p]
        return g_v.at[rows_of(shard, chunk), pl.ds(first_col, cols)]

    def z_copy(p):
        chunk, first_col, cols = PIECES[p]
        mine = grad.at[pl.ds(chunk * CROWS, CROWS), pl.ds(first_col, cols)]
        return rcopy(mine, view(tp, p), z_s.at[p], z_r.at[p], (prv, tp))

    mic = rcopy(mic_out, mic_in, mic_s, mic_r, (prv, tp))
    mic.start()
    for p in range(LAST):
        z_copy(p).start()

    last_rows = grad.at[pl.ds(3 * CROWS, CROWS), :]
    early_to_r = rcopy(last_rows, early_l, er_s, el_r, (pipe, right))
    early_to_l = rcopy(last_rows, early_r, el_s, er_r, (pipe, left))
    early_to_r.start()
    early_to_l.start()
    early_z_l = rcopy(early_l, view(left, LAST), ez_s.at[0], ez_r.at[0], (prv, tp))
    early_z_r = rcopy(early_r, view(right, LAST), ez_s.at[1], ez_r.at[1], (prv, tp))

    loads[0].wait()
    loads[1].wait()

    def attn_copy(slot):
        return rcopy(attn_out.at[slot], attn_in.at[slot], at_s.at[slot], at_r.at[slot], (nxt, tp))

    @pl.loop(0, 4)
    def _(slot):
        row0 = pl.multiple_of(lax.rem(chip + slot + 2, 4) * 128, 128)
        row = lax.broadcasted_iota(jnp.int32, (128, R), 0) + row0
        column = lax.broadcasted_iota(jnp.int32, (128, R), 1)
        begin = jnp.zeros((128, R), jnp.int32)
        for d in range(4):
            begin = jnp.maximum(begin, jnp.where(row >= first[d], first[d], 0))
        bias = jnp.where((column >= begin) & (column <= row), 0.0, MASKED)
        for h in range(4):
            cols = slice(HD * h, HD * h + HD)
            scores = dot_nt(fq_v[pl.ds(row0, 128), cols], fkv_v[0]) + bias
            shifted = jnp.exp2((scores - jnp.max(scores, axis=1, keepdims=True)) * EXP_SCALE)
            total = jnp.sum(shifted, axis=1, keepdims=True)
            attn_out[slot, :, cols] = (dot(shifted.astype(BF16), fkv_v[1]) * (1.0 / total)).astype(BF16)
        attn_copy(slot).start()

    resid_copy = rcopy(resid, resid_in, rs_s, rs_r, (nxt, tp))
    resid_copy.start()
    early_to_r.wait_recv()
    early_z_l.start()
    early_to_l.wait_recv()
    early_z_r.start()
    z_copy(LAST).start()

    loads[2].wait()
    loads[3].wait()
    mic.wait_recv()
    micro = mic_in[0:1, :]
    begins = []
    for d in range(4):
        value = jnp.zeros((1, 128), jnp.int32)
        for m in range(4):
            value = value + jnp.where(micro == m, starts[m, d], 0)
        begins.append(value)

    @pl.loop(0, 4)
    def _(block):
        col0 = pl.multiple_of(block * 128, 128)
        query = lax.broadcasted_iota(jnp.int32, (1, 128), 1) + col0
        begin = jnp.zeros((1, 128), jnp.int32)
        for d in range(4):
            begin = jnp.maximum(begin, jnp.where(query >= begins[d], begins[d], 0))
        key = lax.broadcasted_iota(jnp.int32, (R, 128), 0)
        bias_b[:, pl.ds(col0, 128)] = jnp.where((key >= begin) & (key <= query), 0.0, MASKED)

    kt_v[...] = bkv_v[0].astype(F32).T.astype(BF16)
    vt_v[...] = bkv_v[1].astype(F32).T.astype(BF16)
    dk_v[...] = jnp.zeros_like(dk_v)
    dv_v[...] = jnp.zeros_like(dv_v)

    half_a, half_b = pl.ds(0, HALF), pl.ds(HALF, HALF)

    def to_partner(kind, p, ref):
        return rcopy(ref, ref, p_s.at[kind, p], p_r.at[kind, p], (pipe, partner))

    def x_copies(p, with_chips=True):
        mine = view(tp, p)
        beside = (
            rcopy(mine, mine, xr_s.at[p], fl_r.at[p], (pipe, right)),
            rcopy(mine, mine, xl_s.at[p], fr_r.at[p], (pipe, left)),
        ) if with_chips else ()
        return (*beside, to_partner(0, p, mine))

    def left_copies(p):
        chunk = PIECES[p][0]
        theirs = g_v.at[rows_of(left, chunk), half_a]
        onward = (rcopy(theirs, theirs, yr_s.at[chunk], fl2_r.at[chunk], (pipe, right)),) if p != 1 else ()
        return (*onward, to_partner(1, p, view(left, p)))

    def right_copies(p):
        chunk = PIECES[p][0]
        theirs = g_v.at[rows_of(right, chunk), half_b]
        onward = (rcopy(theirs, theirs, yl_s.at[chunk], fr2_r.at[chunk], (pipe, left)),) if p != 0 else ()
        return (*onward, to_partner(2, p, view(right, p)))

    def opp_copy(k):
        return to_partner(3, k, g_v.at[rows_of(opp, k), :])

    def start_all(copies):
        for copy in copies:
            copy.start()

    def from_next(p):
        landed(view(tp, p), z_r.at[p])
        start_all(x_copies(p))

    def from_sides(p):
        landed(view(left, p), fl_r.at[p])
        start_all(left_copies(p))
        landed(view(right, p), fr_r.at[p])
        start_all(right_copies(p))

    def from_opp(k):
        landed(g_v.at[rows_of(opp, k), half_a], fl2_r.at[k])
        landed(g_v.at[rows_of(opp, k), half_b], fr2_r.at[k])
        opp_copy(k).start()

    def last_left():
        early_z_l.wait_recv()
        start_all(left_copies(LAST))

    def last_right():
        early_z_r.wait_recv()
        start_all(right_copies(LAST))

    def last_own():
        landed(view(tp, LAST), z_r.at[LAST])
        start_all(x_copies(LAST, False))

    @pl.loop(0, 4)
    def _(h):
        @pl.when(h == 0)
        def _():
            from_next(0)

        @pl.when(h == 2)
        def _():
            from_next(1)

        @pl.when(h == 3)
        def _():
            from_sides(0)

        cols = pl.ds(pl.multiple_of(h * HD, HD), HD)
        for b in range(2):
            n = 256 * (b + 1)
            rows = slice(256 * b, n)
            scores = dot_nt(bkv_v[0, :n, :], bq_v[rows, cols]) + bias_b[:n, rows]
            shifted = jnp.exp2((scores - jnp.max(scores, axis=0, keepdims=True)) * EXP_SCALE)
            total = jnp.sum(shifted, axis=0, keepdims=True)
            probs = (shifted * (1.0 / total)).astype(BF16)
            pt_v[h, :n, rows] = probs
            bat_v[cols, rows] = dot(vt_v[:, :n], probs).astype(BF16)

    from_next(2)
    from_sides(1)

    loads[4].wait()

    def project(pair, half):
        lhs = jnp.concatenate([attn_in[slot] for slot in pair], axis=0)

        @pl.loop(4 * half, 4 * half + 4)
        def _(tile):
            cols = pl.ds(pl.multiple_of(tile * TILE, TILE), TILE)
            product = dot(lhs, w_v[:, cols]).astype(BF16)
            for i, slot in enumerate(pair):
                for c in range(2):
                    part[slot, c, :, cols] = product[128 * i + 64 * c : 128 * i + 64 * c + 64, :]

        for slot in pair:
            pp_copy(slot, half).start()

    halves = (half_a, half_b)

    def pp_copy(slot, half):
        return rcopy(
            part.at[slot, 1 - core, :, halves[half]], recvp.at[slot, :, halves[half]],
            pp_s.at[slot, half], pp_r.at[slot, half], (pipe, partner),
        )

    def chip_sum(slot, half, cols):
        begin = half * HALF + cols
        window = pl.ds(pl.multiple_of(begin, TILE), TILE)
        return part[slot, core, :, window].astype(F32) + recvp[slot, :, window].astype(F32)

    def opp_half(half):
        landed(recvp.at[OPP, :, halves[half]], pp_r.at[OPP, half])

        @pl.loop(0, HALF, step=TILE)
        def _(cols):
            opp_sum[half, :, pl.ds(pl.multiple_of(cols, TILE), TILE)] = chip_sum(OPP, half, cols).astype(BF16)

    send_opp_r = rcopy(opp_sum.at[0], rel_l, sr_s.at[0], sl_r.at[0], (pipe, right))
    send_opp_l = rcopy(opp_sum.at[1], rel_r, sl_s.at[0], sr_r.at[0], (pipe, left))
    send_side_l = rcopy(side_sum.at[0], fin_r.at[0], sl_s.at[1], sr_r.at[1], (pipe, left))
    send_side_r = rcopy(side_sum.at[1], fin_l.at[1], sr_s.at[1], sl_r.at[1], (pipe, right))
    send_acc_r = rcopy(acc_r, fin_l.at[0], sr_s.at[2], sl_r.at[2], (pipe, right))
    send_acc_l = rcopy(acc_l, fin_r.at[1], sl_s.at[2], sr_r.at[2], (pipe, left))

    def side_half(slot, half):
        landed(recvp.at[slot, :, halves[half]], pp_r.at[slot, half])

        @pl.loop(0, HALF, step=TILE)
        def _(cols):
            side_sum[half, :, pl.ds(pl.multiple_of(cols, TILE), TILE)] = chip_sum(slot, half, cols).astype(BF16)

    def landed_attn(pair):
        for slot in pair:
            landed(attn_in.at[slot], at_r.at[slot])

    near, far = (OWN, RIGHT), (OPP, LEFT)
    landed_attn(far)
    project(far, 0)
    from_next(3)
    project(far, 1)
    from_sides(2)
    from_opp(0)
    opp_half(0)
    opp_half(1)
    last_left()
    landed_attn(near)
    project(near, 0)
    from_sides(3)
    send_opp_r.start()
    project(near, 1)
    last_right()
    send_opp_l.start()
    side_half(LEFT, 0)
    send_side_l.start()
    from_opp(1)

    peer_shards = [lax.rem(shard, 8) + 1 - 2 * core for shard in (tp, left, right, opp)]

    def attn_grad(half):
        for k in (2 * half, 2 * half + 1):
            for kind, shard in enumerate(peer_shards[:3]):
                for p in range(len(PIECES)):
                    if PIECES[p][0] == k:
                        landed(view(shard, p), p_r.at[kind, p])
            landed(g_v.at[rows_of(peer_shards[3], k), :], p_r.at[3, k])
        acc_v[...] = jnp.zeros_like(acc_v)

        @pl.loop(0, D // DEEP)
        def _(tile):
            cols = pl.ds(pl.multiple_of(tile * DEEP, DEEP), DEEP)
            lhs = jnp.concatenate([g_v[64 * i + 32 * half : 64 * i + 32 * half + 32, cols] for i in range(8)], axis=0)
            acc_v[...] += dot_nt(lhs, w_v[:, cols])

        for i in range(8):
            ga_v[64 * i + 32 * half : 64 * i + 32 * half + 32, :] = acc_v[32 * i : 32 * i + 32, :].astype(BF16)

    attn_grad(0)
    side_half(RIGHT, 1)
    send_side_r.start()
    last_own()
    from_opp(2)
    from_opp(3)
    attn_grad(1)

    def gw_copy(tile):
        cols = pl.ds(pl.multiple_of(tile * TILE, TILE), TILE)
        return pltpu.make_async_copy(gw_v.at[:, cols], gw.at[:, cols], gw_sem.at[tile])

    def weight_grad(half):
        @pl.loop(4 * half, 4 * half + 4)
        def _(tile):
            cols = pl.ds(pl.multiple_of(tile * TILE, TILE), TILE)
            gw_v[:, cols] = dot(bat_v[...], g_v[:, cols]).astype(BF16)
            gw_copy(tile).start()

    weight_grad(0)

    landed(rel_l, sl_r.at[0])
    landed(recvp.at[RIGHT, :, half_a], pp_r.at[RIGHT, 0])
    landed(rel_r, sr_r.at[0])
    landed(recvp.at[LEFT, :, half_b], pp_r.at[LEFT, 1])

    @pl.loop(0, HALF, step=TILE)
    def _(cols):
        window = pl.ds(pl.multiple_of(cols, TILE), TILE)
        acc_r[:, window] = (chip_sum(RIGHT, 0, cols) + rel_l[:, window].astype(F32)).astype(BF16)
        acc_l[:, window] = (chip_sum(LEFT, 1, cols) + rel_r[:, window].astype(F32)).astype(BF16)

    send_acc_r.start()
    send_acc_l.start()

    weight_grad(1)

    @pl.loop(0, 4)
    def _(h):
        cols = pl.ds(pl.multiple_of(h * HD, HD), HD)
        for b in range(2):
            n = 256 * (b + 1)
            rows = slice(256 * b, n)
            grad_rows = ga_v[rows, cols]
            dprob = dot_nt(bkv_v[1, :n, :], grad_rows)
            probs = pt_v[h, :n, rows]
            wide = probs.astype(F32)
            delta = jnp.sum(wide * dprob, axis=0, keepdims=True)
            dscore = (wide * (dprob - delta) * SCALE).astype(BF16)
            gq_v[rows, cols] = dot(kt_v[:, :n], dscore).T.astype(BF16)
            dk_v[:n, :] += dot(dscore, bq_v[rows, cols])
            dv_v[:n, :] += dot(probs, grad_rows)

    gkv_v[0] = dk_v[...].astype(BF16)
    gkv_v[1] = dv_v[...].astype(BF16)
    stores = [pltpu.make_async_copy(gq_v, gq, st_sem.at[0]), pltpu.make_async_copy(gkv_v, gkv, st_sem.at[1])]
    for store in stores:
        store.start()

    resid_copy.wait_recv()
    for half in range(2):
        landed(recvp.at[OWN, :, halves[half]], pp_r.at[OWN, half])
        landed(fin_l.at[half], sl_r.at[2 if half == 0 else 1])
        landed(fin_r.at[half], sr_r.at[1 if half == 0 else 2])

        @pl.loop(0, HALF, step=TILE)
        def _(cols):
            window = pl.ds(pl.multiple_of(cols, TILE), TILE)
            place = pl.ds(pl.multiple_of(half * HALF + cols, TILE), TILE)
            total = chip_sum(OWN, half, cols) + fin_l[half, :, window].astype(F32) + fin_r[half, :, window].astype(F32)
            out_v[:, place] = (resid_in[:, place].astype(F32) + total).astype(BF16)

        store = pltpu.make_async_copy(out_v.at[:, halves[half]], out.at[:, halves[half]], st_sem.at[2 + half])
        store.start()
        stores.append(store)

    mic.wait_send()
    resid_copy.wait_send()
    for h in range(4):
        attn_copy(h).wait_send()
    for copy in (early_to_r, early_to_l, early_z_l, early_z_r):
        copy.wait_send()
    for p in range(len(PIECES)):
        for copy in (z_copy(p), *x_copies(p, p < LAST), *left_copies(p), *right_copies(p)):
            copy.wait_send()
    for k in range(CHUNKS):
        opp_copy(k).wait_send()
    for slot in range(4):
        for half in range(2):
            pp_copy(slot, half).wait_send()
    for copy in (send_opp_r, send_opp_l, send_side_l, send_side_r, send_acc_r, send_acc_l):
        copy.wait_send()
    for tile in range(D // TILE):
        gw_copy(tile).wait()
    for store in stores:
        store.wait()


def deliver(*refs):
    srcs, dsts, sem = refs[:4], refs[4:8], refs[8]
    pieces = []
    for src, dst in zip(srcs, dsts):
        rows = src.shape[-2]
        for lead in range(src.shape[0]):
            for row in range(0, rows, 64):
                pieces.append(tuple(ref.at[lead, pl.ds(row, 64), :] for ref in (src, dst)))
    copies = [pltpu.make_async_copy(a, b, sem.at[i]) for i, (a, b) in enumerate(pieces)]
    for copy in copies:
        copy.start()
    for copy in copies:
        copy.wait()


def shards(fwd_resid, fwd_query, fwd_keyval, fwd_micro, bwd_query, bwd_keyval, grad_micro, grad_in, out_weight, doc_starts):
    any_space = pl.BlockSpec(memory_space=pl.ANY)
    smem = pl.BlockSpec(memory_space=pltpu.SMEM)
    dma = pltpu.SemaphoreType.DMA
    vmem = pltpu.VMEM
    scratch = [
        vmem((R, R), BF16), vmem((2, R, HD), BF16), vmem((R, R), BF16), vmem((2, R, HD), BF16),
        vmem((R, D), BF16), vmem((R, D), BF16),
        vmem((4, HD, R), BF16), vmem((4, HD, R), BF16), vmem((64, D), BF16),
        vmem((8, 128), jnp.int32), vmem((8, 128), jnp.int32),
        vmem((R, R), F32), vmem((HD, R), BF16), vmem((HD, R), BF16),
        vmem((4, R, R), BF16), vmem((R, R), BF16), vmem((R // 2, R), F32), vmem((R, R), BF16),
        vmem((R, HD), F32), vmem((R, HD), F32), vmem((R, R), BF16), vmem((2, R, HD), BF16), vmem((R, D), BF16),
        vmem((4, 2, 64, D), BF16), vmem((4, 64, D), BF16), vmem((2, 64, HALF), BF16), vmem((2, 64, HALF), BF16),
        vmem((64, HALF), BF16), vmem((64, HALF), BF16), vmem((2, 64, HALF), BF16), vmem((2, 64, HALF), BF16),
        vmem((64, HALF), BF16), vmem((64, HALF), BF16), vmem((64, D), BF16),
        dma((5,)), dma((4,)), dma((D // TILE,)),
        vmem((CROWS, D), BF16), vmem((CROWS, D), BF16), dma, dma, dma, dma, dma((2,)), dma((2,)),
        dma((len(PIECES),)), dma((len(PIECES),)), dma, dma, dma((4,)), dma((4,)), dma, dma,
        dma((LAST,)), dma((LAST,)), dma((LAST,)), dma((LAST,)),
        dma((CHUNKS,)), dma((CHUNKS,)), dma((CHUNKS,)), dma((CHUNKS,)),
        dma((4, len(PIECES))), dma((4, len(PIECES))),
        dma((4, 2)), dma((4, 2)), dma((3,)), dma((3,)), dma((3,)), dma((3,)),
    ]
    out, gq, gkv, gw = pl.pallas_call(
        kernel,
        out_shape=(
            jax.ShapeDtypeStruct((64, D), BF16),
            jax.ShapeDtypeStruct((R, R), BF16),
            jax.ShapeDtypeStruct((2, R, HD), BF16),
            jax.ShapeDtypeStruct((R, D), BF16),
        ),
        in_specs=[smem] * 3 + [pl.BlockSpec(memory_space=pltpu.HBM)] * 7,
        out_specs=(any_space,) * 4,
        scratch_shapes=scratch,
        compiler_params=pltpu.CompilerParams(
            collective_id=0, has_side_effects=True, vmem_limit_bytes=40 * 1024 * 1024
        ),
    )(
        fwd_micro, grad_micro, pltpu.with_memory_space_constraint(doc_starts, pltpu.HBM),
        *(
            pltpu.with_memory_space_constraint(a[0], pltpu.HBM)
            for a in (fwd_resid, fwd_query, fwd_keyval, bwd_query, bwd_keyval, grad_in, out_weight)
        ),
    )
    arrays = (gw[None], gq[None], gkv, out[None])
    count = sum(a.shape[0] * max(a.shape[1] // 64, 1) for a in arrays)
    gw, gq, gkv, out = pl.pallas_call(
        deliver,
        out_shape=tuple(jax.ShapeDtypeStruct(a.shape, a.dtype) for a in arrays),
        in_specs=[any_space] * 4,
        out_specs=(any_space,) * 4,
        scratch_shapes=[dma((count,))],
        compiler_params=pltpu.CompilerParams(vmem_limit_bytes=4 * 1024 * 1024),
    )(*arrays)
    return (out, gq, gkv[None], gw)


def solution(mesh):
    return jax.shard_map(
        shards,
        mesh=mesh,
        in_specs=(
            P("pipe", "tp", None),
            P("pipe", None, "tp"),
            P("pipe", None, None, "tp"),
            P("pipe"),
            P("pipe", None, "tp"),
            P("pipe", None, None, "tp"),
            P("pipe"),
            P("pipe", "tp", None),
            P("pipe", "tp", None),
            P(),
        ),
        out_specs=(
            P("pipe", "tp", None),
            P("pipe", None, "tp"),
            P("pipe", None, None, "tp"),
            P("pipe", "tp", None),
        ),
        check_vma=False,
    )
```

```python
import functools
import math

import jax
import jax.numpy as jnp
from jax import lax
from jax.experimental import pallas as pl
from jax.experimental.pallas import tpu as pltpu
from jax.sharding import PartitionSpec as P

MESH = pl.DeviceIdType.MESH
F32 = jnp.float32
BF16 = jnp.bfloat16
R = 512
D = 4096
HD = 128
HALF = D // 2
SCALE = 1.0 / math.sqrt(HD)
EXP_SCALE = SCALE * math.log2(math.e)
MASKED = -1e30
CHUNKS = 4
CROWS = 64 // CHUNKS
TILE = 512
DEEP = 1024
PIECES = ((0, 0, HALF), (0, HALF, HALF), (1, 0, D), (2, 0, D), (3, 0, D))
LAST = len(PIECES) - 1
OPP, LEFT, OWN, RIGHT = 0, 1, 2, 3


def dot(a, b):
    return jnp.dot(a, b, preferred_element_type=F32)


def dot_nt(a, b):
    return lax.dot_general(a, b, (((1,), (1,)), ((), ())), preferred_element_type=F32)


def kernel(
    fwd_micro, grad_micro, starts_h, resid, fq, fkv, bq, bkv, grad, weight,
    out, gq, gkv, gw,
    starts, fq_v, fkv_v, bq_v, bkv_v, w_v, g_v, attn_out, attn_in, resid_in, mic_out, mic_in,
    bias_b, kt_v, vt_v, pt_v, bat_v, acc_v, ga_v, dk_v, dv_v, gq_v, gkv_v, gw_v,
    part, recvp, opp_sum, side_sum, rel_l, rel_r, fin_l, fin_r, acc_r, acc_l, out_v,
    ld_sem, st_sem, gw_sem,
    early_l, early_r, early_o, el_s, el_r, er_s, er_r, eo_s, eo_r, ez_s, ez_r,
    z_s, z_r, mic_s, mic_r, at_s, at_r, rs_s, rs_r,
    xr_s, xl_s, fl_r, fr_r, yr_s, yl_s, fl2_r, fr2_r, p_s, p_r,
    pp_s, pp_r, sr_s, sl_s, sl_r, sr_r,
):
    pipe, tp = lax.axis_index("pipe"), lax.axis_index("tp")
    n_pipe = lax.axis_size("pipe")
    core = lax.rem(tp, 2)
    partner = tp + 1 - 2 * core
    right, left, opp = lax.rem(tp + 2, 8), lax.rem(tp + 6, 8), lax.rem(tp + 4, 8)
    chip = lax.div(tp, 2)
    nxt, prv = lax.rem(pipe + 1, n_pipe), lax.rem(pipe + n_pipe - 1, n_pipe)

    def rcopy(src, dst, send, recv, device):
        return pltpu.make_async_remote_copy(
            src_ref=src, dst_ref=dst, send_sem=send, recv_sem=recv, device_id=device, device_id_type=MESH
        )

    def landed(dst, recv):
        pltpu.make_async_copy(dst, dst, recv).wait()

    loads = [
        pltpu.make_async_copy(src, dst, ld_sem.at[i])
        for i, (src, dst) in enumerate(
            [
                (fkv, fkv_v), (fq, fq_v), (bkv, bkv_v), (bq, bq_v), (weight, w_v),
                (starts_h, starts),
            ]
        )
    ]
    barrier = pltpu.get_barrier_semaphore()
    peers = ((pipe, partner), (pipe, right), (pipe, left), (nxt, tp), (prv, tp))
    for peer in peers:
        pl.semaphore_signal(barrier, inc=1, device_id=peer, device_id_type=MESH)
    for load in (*loads[5:], *loads[:5]):
        load.start()
    for load in loads[5:]:
        load.wait()
    mic_out[...] = jnp.full(mic_out.shape, grad_micro[0], jnp.int32)

    first = [starts[0, d] for d in range(4)]
    for m in range(1, 4):
        first = [jnp.where(fwd_micro[0] == m, starts[m, d], first[d]) for d in range(4)]

    pl.semaphore_wait(barrier, len(peers))

    def rows_of(shard, k):
        return pl.ds(pl.multiple_of(shard * 64 + k * CROWS, CROWS), CROWS)

    def view(shard, p):
        chunk, first_col, cols = PIECES[p]
        return g_v.at[rows_of(shard, chunk), pl.ds(first_col, cols)]

    def z_copy(p):
        chunk, first_col, cols = PIECES[p]
        mine = grad.at[pl.ds(chunk * CROWS, CROWS), pl.ds(first_col, cols)]
        return rcopy(mine, view(tp, p), z_s.at[p], z_r.at[p], (prv, tp))

    mic = rcopy(mic_out, mic_in, mic_s, mic_r, (prv, tp))
    mic.start()
    for p in range(LAST):
        z_copy(p).start()

    last_rows = grad.at[pl.ds(3 * CROWS, CROWS), :]
    early_to_r = rcopy(last_rows, early_l, er_s, el_r, (pipe, right))
    early_to_l = rcopy(last_rows, early_r, el_s, er_r, (pipe, left))
    early_to_r.start()
    early_to_l.start()
    early_z_l = rcopy(early_l, view(left, LAST), ez_s.at[0], ez_r.at[0], (prv, tp))
    early_z_r = rcopy(early_r, view(right, LAST), ez_s.at[1], ez_r.at[1], (prv, tp))
    early_z_o = rcopy(early_o, view(opp, LAST), ez_s.at[2], ez_r.at[2], (prv, tp))
    half_a, half_b = pl.ds(0, HALF), pl.ds(HALF, HALF)
    onward_r = rcopy(early_l.at[:, half_a], early_o.at[:, half_a], eo_s.at[0], eo_r.at[0], (pipe, right))
    onward_l = rcopy(early_r.at[:, half_b], early_o.at[:, half_b], eo_s.at[1], eo_r.at[1], (pipe, left))

    loads[0].wait()
    loads[1].wait()

    def attn_copy(slot):
        return rcopy(attn_out.at[slot], attn_in.at[slot], at_s.at[slot], at_r.at[slot], (nxt, tp))

    @pl.loop(0, 4)
    def _(slot):
        row0 = pl.multiple_of(lax.rem(chip + slot + 2, 4) * 128, 128)
        row = lax.broadcasted_iota(jnp.int32, (128, R), 0) + row0
        column = lax.broadcasted_iota(jnp.int32, (128, R), 1)
        begin = jnp.zeros((128, R), jnp.int32)
        for d in range(4):
            begin = jnp.maximum(begin, jnp.where(row >= first[d], first[d], 0))
        bias = jnp.where((column >= begin) & (column <= row), 0.0, MASKED)
        for h in range(4):
            cols = slice(HD * h, HD * h + HD)
            scores = dot_nt(fq_v[pl.ds(row0, 128), cols], fkv_v[0]) + bias
            shifted = jnp.exp2((scores - jnp.max(scores, axis=1, keepdims=True)) * EXP_SCALE)
            total = jnp.sum(shifted, axis=1, keepdims=True)
            attn_out[slot, :, cols] = (dot(shifted.astype(BF16), fkv_v[1]) * (1.0 / total)).astype(BF16)
        attn_copy(slot).start()

    resid_copy = rcopy(resid, resid_in, rs_s, rs_r, (nxt, tp))
    resid_copy.start()
    loads[2].wait()
    loads[3].wait()
    mic.wait_recv()
    micro = mic_in[0:1, :]
    begins = []
    for d in range(4):
        value = jnp.zeros((1, 128), jnp.int32)
        for m in range(4):
            value = value + jnp.where(micro == m, starts[m, d], 0)
        begins.append(value)

    @pl.loop(0, 4)
    def _(block):
        col0 = pl.multiple_of(block * 128, 128)
        query = lax.broadcasted_iota(jnp.int32, (1, 128), 1) + col0
        begin = jnp.zeros((1, 128), jnp.int32)
        for d in range(4):
            begin = jnp.maximum(begin, jnp.where(query >= begins[d], begins[d], 0))
        key = lax.broadcasted_iota(jnp.int32, (R, 128), 0)
        bias_b[:, pl.ds(col0, 128)] = jnp.where((key >= begin) & (key <= query), 0.0, MASKED)

    kt_v[...] = bkv_v[0].astype(F32).T.astype(BF16)
    vt_v[...] = bkv_v[1].astype(F32).T.astype(BF16)
    dk_v[...] = jnp.zeros_like(dk_v)
    dv_v[...] = jnp.zeros_like(dv_v)

    def to_partner(kind, p, ref):
        return rcopy(ref, ref, p_s.at[kind, p], p_r.at[kind, p], (pipe, partner))

    def x_copies(p, with_chips=True):
        mine = view(tp, p)
        beside = (
            rcopy(mine, mine, xr_s.at[p], fl_r.at[p], (pipe, right)),
            rcopy(mine, mine, xl_s.at[p], fr_r.at[p], (pipe, left)),
        ) if with_chips else ()
        return (*beside, to_partner(0, p, mine))

    def left_copies(p):
        chunk = PIECES[p][0]
        theirs = g_v.at[rows_of(left, chunk), half_a]
        onward = (rcopy(theirs, theirs, yr_s.at[chunk], fl2_r.at[chunk], (pipe, right)),) if p not in (1, LAST) else ()
        return (*onward, to_partner(1, p, view(left, p)))

    def right_copies(p):
        chunk = PIECES[p][0]
        theirs = g_v.at[rows_of(right, chunk), half_b]
        onward = (rcopy(theirs, theirs, yl_s.at[chunk], fr2_r.at[chunk], (pipe, left)),) if p not in (0, LAST) else ()
        return (*onward, to_partner(2, p, view(right, p)))

    def opp_copy(k):
        return to_partner(3, k, g_v.at[rows_of(opp, k), :])

    def start_all(copies):
        for copy in copies:
            copy.start()

    def from_next(p):
        landed(view(tp, p), z_r.at[p])
        start_all(x_copies(p))

    def from_sides(p):
        landed(view(left, p), fl_r.at[p])
        start_all(left_copies(p))
        landed(view(right, p), fr_r.at[p])
        start_all(right_copies(p))

    def from_opp(k):
        landed(g_v.at[rows_of(opp, k), half_a], fl2_r.at[k])
        landed(g_v.at[rows_of(opp, k), half_b], fr2_r.at[k])
        opp_copy(k).start()

    def last_left():
        early_z_l.wait_recv()
        start_all(left_copies(LAST))

    def last_right():
        early_z_r.wait_recv()
        start_all(right_copies(LAST))

    def last_opp():
        early_z_o.wait_recv()
        opp_copy(CHUNKS - 1).start()

    def last_own():
        landed(view(tp, LAST), z_r.at[LAST])
        start_all(x_copies(LAST, False))

    @pl.loop(0, 4)
    def _(h):
        @pl.when(h == 0)
        def _():
            from_next(0)

        @pl.when(h == 1)
        def _():
            early_to_r.wait_recv()
            onward_r.start()
            early_z_l.start()
            early_to_l.wait_recv()
            onward_l.start()
            early_z_r.start()
            z_copy(LAST).start()

        @pl.when(h == 2)
        def _():
            from_next(1)

        cols = pl.ds(pl.multiple_of(h * HD, HD), HD)
        for b in range(2):
            n = 256 * (b + 1)
            rows = slice(256 * b, n)
            scores = dot_nt(bkv_v[0, :n, :], bq_v[rows, cols]) + bias_b[:n, rows]
            shifted = jnp.exp2((scores - jnp.max(scores, axis=0, keepdims=True)) * EXP_SCALE)
            total = jnp.sum(shifted, axis=0, keepdims=True)
            probs = (shifted * (1.0 / total)).astype(BF16)
            pt_v[h, :n, rows] = probs
            bat_v[cols, rows] = dot(vt_v[:, :n], probs).astype(BF16)

    from_next(2)
    from_sides(0)
    from_sides(1)
    from_next(3)

    loads[4].wait()

    def project(pair, half):
        lhs = jnp.concatenate([attn_in[slot] for slot in pair], axis=0)

        @pl.loop(4 * half, 4 * half + 4)
        def _(tile):
            cols = pl.ds(pl.multiple_of(tile * TILE, TILE), TILE)
            product = dot(lhs, w_v[:, cols]).astype(BF16)
            for i, slot in enumerate(pair):
                for c in range(2):
                    part[slot, c, :, cols] = product[128 * i + 64 * c : 128 * i + 64 * c + 64, :]

        for slot in pair:
            pp_copy(slot, half).start()

    halves = (half_a, half_b)

    def pp_copy(slot, half):
        return rcopy(
            part.at[slot, 1 - core, :, halves[half]], recvp.at[slot, :, halves[half]],
            pp_s.at[slot, half], pp_r.at[slot, half], (pipe, partner),
        )

    def chip_sum(slot, half, cols):
        begin = half * HALF + cols
        window = pl.ds(pl.multiple_of(begin, TILE), TILE)
        return part[slot, core, :, window].astype(F32) + recvp[slot, :, window].astype(F32)

    def opp_half(half):
        landed(recvp.at[OPP, :, halves[half]], pp_r.at[OPP, half])

        @pl.loop(0, HALF, step=TILE)
        def _(cols):
            opp_sum[half, :, pl.ds(pl.multiple_of(cols, TILE), TILE)] = chip_sum(OPP, half, cols).astype(BF16)

    send_opp_r = rcopy(opp_sum.at[0], rel_l, sr_s.at[0], sl_r.at[0], (pipe, right))
    send_opp_l = rcopy(opp_sum.at[1], rel_r, sl_s.at[0], sr_r.at[0], (pipe, left))
    send_side_l = rcopy(side_sum.at[0], fin_r.at[0], sl_s.at[1], sr_r.at[1], (pipe, left))
    send_side_r = rcopy(side_sum.at[1], fin_l.at[1], sr_s.at[1], sl_r.at[1], (pipe, right))
    send_acc_r = rcopy(acc_r, fin_l.at[0], sr_s.at[2], sl_r.at[2], (pipe, right))
    send_acc_l = rcopy(acc_l, fin_r.at[1], sl_s.at[2], sr_r.at[2], (pipe, left))

    def side_half(slot, half):
        landed(recvp.at[slot, :, halves[half]], pp_r.at[slot, half])

        @pl.loop(0, HALF, step=TILE)
        def _(cols):
            side_sum[half, :, pl.ds(pl.multiple_of(cols, TILE), TILE)] = chip_sum(slot, half, cols).astype(BF16)

    def landed_attn(pair):
        for slot in pair:
            landed(attn_in.at[slot], at_r.at[slot])

    near, far = (OWN, RIGHT), (OPP, LEFT)
    landed_attn(far)
    project(far, 0)
    onward_r.wait_recv()
    onward_l.wait_recv()
    early_z_o.start()
    project(far, 1)
    from_sides(2)
    from_opp(0)
    opp_half(0)
    opp_half(1)
    last_left()
    landed_attn(near)
    project(near, 0)
    from_sides(3)
    send_opp_r.start()
    project(near, 1)
    last_right()
    send_opp_l.start()
    side_half(LEFT, 0)
    send_side_l.start()
    from_opp(1)

    peer_shards = [lax.rem(shard, 8) + 1 - 2 * core for shard in (tp, left, right, opp)]

    def attn_grad(half):
        for k in (2 * half, 2 * half + 1):
            for kind, shard in enumerate(peer_shards[:3]):
                for p in range(len(PIECES)):
                    if PIECES[p][0] == k:
                        landed(view(shard, p), p_r.at[kind, p])
            landed(g_v.at[rows_of(peer_shards[3], k), :], p_r.at[3, k])
        acc_v[...] = jnp.zeros_like(acc_v)

        @pl.loop(0, D // DEEP)
        def _(tile):
            cols = pl.ds(pl.multiple_of(tile * DEEP, DEEP), DEEP)
            lhs = jnp.concatenate([g_v[64 * i + 32 * half : 64 * i + 32 * half + 32, cols] for i in range(8)], axis=0)
            acc_v[...] += dot_nt(lhs, w_v[:, cols])

        for i in range(8):
            ga_v[64 * i + 32 * half : 64 * i + 32 * half + 32, :] = acc_v[32 * i : 32 * i + 32, :].astype(BF16)


    @pl.when(core == 1)
    def _():
        from_opp(2)
        last_own()

    side_half(RIGHT, 1)
    send_side_r.start()
    attn_grad(0)

    @pl.when(core == 0)
    def _():
        last_own()
        from_opp(2)

    last_opp()
    attn_grad(1)

    def gw_copy(tile):
        cols = pl.ds(pl.multiple_of(tile * TILE, TILE), TILE)
        return pltpu.make_async_copy(gw_v.at[:, cols], gw.at[:, cols], gw_sem.at[tile])

    def weight_grad(first_tile, stop):
        @pl.loop(first_tile, stop)
        def _(tile):
            cols = pl.ds(pl.multiple_of(tile * TILE, TILE), TILE)
            gw_v[:, cols] = dot(bat_v[...], g_v[:, cols]).astype(BF16)
            gw_copy(tile).start()

    weight_grad(0, 4)

    landed(rel_l, sl_r.at[0])
    landed(recvp.at[RIGHT, :, half_a], pp_r.at[RIGHT, 0])
    landed(rel_r, sr_r.at[0])
    landed(recvp.at[LEFT, :, half_b], pp_r.at[LEFT, 1])

    @pl.loop(0, HALF, step=TILE)
    def _(cols):
        window = pl.ds(pl.multiple_of(cols, TILE), TILE)
        acc_r[:, window] = (chip_sum(RIGHT, 0, cols) + rel_l[:, window].astype(F32)).astype(BF16)
        acc_l[:, window] = (chip_sum(LEFT, 1, cols) + rel_r[:, window].astype(F32)).astype(BF16)

    send_acc_r.start()
    send_acc_l.start()

    weight_grad(4, D // TILE)

    @pl.loop(0, 4)
    def _(h):
        cols = pl.ds(pl.multiple_of(h * HD, HD), HD)
        for b in range(2):
            n = 256 * (b + 1)
            rows = slice(256 * b, n)
            grad_rows = ga_v[rows, cols]
            dprob = dot_nt(bkv_v[1, :n, :], grad_rows)
            probs = pt_v[h, :n, rows]
            wide = probs.astype(F32)
            delta = jnp.sum(wide * dprob, axis=0, keepdims=True)
            dscore = (wide * (dprob - delta) * SCALE).astype(BF16)
            gq_v[rows, cols] = dot(kt_v[:, :n], dscore).T.astype(BF16)
            dk_v[:n, :] += dot(dscore, bq_v[rows, cols])
            dv_v[:n, :] += dot(probs, grad_rows)

    gkv_v[0] = dk_v[...].astype(BF16)
    gkv_v[1] = dv_v[...].astype(BF16)
    stores = [pltpu.make_async_copy(gq_v, gq, st_sem.at[0]), pltpu.make_async_copy(gkv_v, gkv, st_sem.at[1])]
    for store in stores:
        store.start()

    resid_copy.wait_recv()
    for half in range(2):
        landed(recvp.at[OWN, :, halves[half]], pp_r.at[OWN, half])
        landed(fin_l.at[half], sl_r.at[2 if half == 0 else 1])
        landed(fin_r.at[half], sr_r.at[1 if half == 0 else 2])

        @pl.loop(0, HALF, step=TILE)
        def _(cols):
            window = pl.ds(pl.multiple_of(cols, TILE), TILE)
            place = pl.ds(pl.multiple_of(half * HALF + cols, TILE), TILE)
            total = chip_sum(OWN, half, cols) + fin_l[half, :, window].astype(F32) + fin_r[half, :, window].astype(F32)
            out_v[:, place] = (resid_in[:, place].astype(F32) + total).astype(BF16)

        store = pltpu.make_async_copy(out_v.at[:, halves[half]], out.at[:, halves[half]], st_sem.at[2 + half])
        store.start()
        stores.append(store)

    mic.wait_send()
    resid_copy.wait_send()
    for h in range(4):
        attn_copy(h).wait_send()
    for copy in (early_to_r, early_to_l, onward_r, onward_l, early_z_l, early_z_r, early_z_o):
        copy.wait_send()
    for p in range(len(PIECES)):
        for copy in (z_copy(p), *x_copies(p, p < LAST), *left_copies(p), *right_copies(p)):
            copy.wait_send()
    for k in range(CHUNKS):
        opp_copy(k).wait_send()
    for slot in range(4):
        for half in range(2):
            pp_copy(slot, half).wait_send()
    for copy in (send_opp_r, send_opp_l, send_side_l, send_side_r, send_acc_r, send_acc_l):
        copy.wait_send()
    for tile in range(D // TILE):
        gw_copy(tile).wait()
    for store in stores:
        store.wait()


def deliver(*refs):
    srcs, dsts, sem = refs[:4], refs[4:8], refs[8]
    pieces = []
    for src, dst in zip(srcs, dsts):
        rows = src.shape[-2]
        for lead in range(src.shape[0]):
            for row in range(0, rows, 64):
                pieces.append(tuple(ref.at[lead, pl.ds(row, 64), :] for ref in (src, dst)))
    copies = [pltpu.make_async_copy(a, b, sem.at[i]) for i, (a, b) in enumerate(pieces)]
    for copy in copies:
        copy.start()
    for copy in copies:
        copy.wait()


def shards(fwd_resid, fwd_query, fwd_keyval, fwd_micro, bwd_query, bwd_keyval, grad_micro, grad_in, out_weight, doc_starts):
    any_space = pl.BlockSpec(memory_space=pl.ANY)
    smem = pl.BlockSpec(memory_space=pltpu.SMEM)
    dma = pltpu.SemaphoreType.DMA
    vmem = pltpu.VMEM
    scratch = [
        pltpu.SMEM((4, 4), jnp.int32),
        vmem((R, R), BF16), vmem((2, R, HD), BF16), vmem((R, R), BF16), vmem((2, R, HD), BF16),
        vmem((R, D), BF16), vmem((R, D), BF16),
        vmem((4, HD, R), BF16), vmem((4, HD, R), BF16), vmem((64, D), BF16),
        vmem((8, 128), jnp.int32), vmem((8, 128), jnp.int32),
        vmem((R, R), F32), vmem((HD, R), BF16), vmem((HD, R), BF16),
        vmem((4, R, R), BF16), vmem((R, R), BF16), vmem((R // 2, R), F32), vmem((R, R), BF16),
        vmem((R, HD), F32), vmem((R, HD), F32), vmem((R, R), BF16), vmem((2, R, HD), BF16), vmem((R, D), BF16),
        vmem((4, 2, 64, D), BF16), vmem((4, 64, D), BF16), vmem((2, 64, HALF), BF16), vmem((2, 64, HALF), BF16),
        vmem((64, HALF), BF16), vmem((64, HALF), BF16), vmem((2, 64, HALF), BF16), vmem((2, 64, HALF), BF16),
        vmem((64, HALF), BF16), vmem((64, HALF), BF16), vmem((64, D), BF16),
        dma((6,)), dma((4,)), dma((D // TILE,)),
        vmem((CROWS, D), BF16), vmem((CROWS, D), BF16), vmem((CROWS, D), BF16),
        dma, dma, dma, dma, dma((2,)), dma((2,)), dma((3,)), dma((3,)),
        dma((len(PIECES),)), dma((len(PIECES),)), dma, dma, dma((4,)), dma((4,)), dma, dma,
        dma((LAST,)), dma((LAST,)), dma((LAST,)), dma((LAST,)),
        dma((CHUNKS,)), dma((CHUNKS,)), dma((CHUNKS,)), dma((CHUNKS,)),
        dma((4, len(PIECES))), dma((4, len(PIECES))),
        dma((4, 2)), dma((4, 2)), dma((3,)), dma((3,)), dma((3,)), dma((3,)),
    ]
    out, gq, gkv, gw = pl.pallas_call(
        kernel,
        out_shape=(
            jax.ShapeDtypeStruct((64, D), BF16),
            jax.ShapeDtypeStruct((R, R), BF16),
            jax.ShapeDtypeStruct((2, R, HD), BF16),
            jax.ShapeDtypeStruct((R, D), BF16),
        ),
        in_specs=[smem] * 2 + [pl.BlockSpec(memory_space=pltpu.HBM)] * 8,
        out_specs=(any_space,) * 4,
        scratch_shapes=scratch,
        compiler_params=pltpu.CompilerParams(
            collective_id=0, has_side_effects=True, vmem_limit_bytes=40 * 1024 * 1024
        ),
    )(
        fwd_micro, grad_micro, pltpu.with_memory_space_constraint(doc_starts, pltpu.HBM),
        *(
            pltpu.with_memory_space_constraint(a[0], pltpu.HBM)
            for a in (fwd_resid, fwd_query, fwd_keyval, bwd_query, bwd_keyval, grad_in, out_weight)
        ),
    )
    arrays = (gw[None], gq[None], gkv, out[None])
    count = sum(a.shape[0] * max(a.shape[1] // 64, 1) for a in arrays)
    gw, gq, gkv, out = pl.pallas_call(
        deliver,
        out_shape=tuple(jax.ShapeDtypeStruct(a.shape, a.dtype) for a in arrays),
        in_specs=[any_space] * 4,
        out_specs=(any_space,) * 4,
        scratch_shapes=[dma((count,))],
        compiler_params=pltpu.CompilerParams(vmem_limit_bytes=4 * 1024 * 1024),
    )(*arrays)
    return (out, gq, gkv[None], gw)


def solution(mesh):
    return jax.shard_map(
        shards,
        mesh=mesh,
        in_specs=(
            P("pipe", "tp", None),
            P("pipe", None, "tp"),
            P("pipe", None, None, "tp"),
            P("pipe"),
            P("pipe", None, "tp"),
            P("pipe", None, None, "tp"),
            P("pipe"),
            P("pipe", "tp", None),
            P("pipe", "tp", None),
            P(),
        ),
        out_specs=(
            P("pipe", "tp", None),
            P("pipe", None, "tp"),
            P("pipe", None, None, "tp"),
            P("pipe", "tp", None),
        ),
        check_vma=False,
    )
```

```python
import functools
import math

import jax
import jax.numpy as jnp
from jax import lax
from jax.experimental import pallas as pl
from jax.experimental.pallas import tpu as pltpu
from jax.sharding import PartitionSpec as P

MESH = pl.DeviceIdType.MESH
F32 = jnp.float32
BF16 = jnp.bfloat16
R = 512
D = 4096
HD = 128
HALF = D // 2
SCALE = 1.0 / math.sqrt(HD)
EXP_SCALE = SCALE * math.log2(math.e)
MASKED = -1e30
CHUNKS = 4
CROWS = 64 // CHUNKS
TILE = 512
DEEP = 1024
PIECES = ((0, 0, HALF), (0, HALF, HALF), (1, 0, D), (2, 0, D), (3, 0, D))
LAST = len(PIECES) - 1
OPP, LEFT, OWN, RIGHT = 0, 1, 2, 3


def dot(a, b):
    return jnp.dot(a, b, preferred_element_type=F32)


def dot_nt(a, b):
    return lax.dot_general(a, b, (((1,), (1,)), ((), ())), preferred_element_type=F32)


def kernel(
    fwd_micro, grad_micro, starts_h, resid, fq, fkv, bq, bkv, grad, weight,
    base, gq, gkv, gw, fin_l, fin_r,
    starts, fq_v, fkv_v, bq_v, bkv_v, w_v, g_v, attn_out, attn_in, resid_in, mic_out, mic_in,
    bias_b, kt_v, vt_v, pt_v, bat_v, acc_v, ga_v, dk_v, dv_v, gq_v, gkv_v, gw_v,
    part, recvp, opp_sum, side_sum, rel_l, rel_r, acc_r, acc_l, base_v,
    ld_sem, st_sem, gw_sem,
    early_l, early_r, early_o, el_s, el_r, er_s, er_r, eo_s, eo_r, ez_s, ez_r,
    z_s, z_r, mic_s, mic_r, at_s, at_r, rs_s, rs_r,
    xr_s, xl_s, fl_r, fr_r, yr_s, yl_s, fl2_r, fr2_r, p_s, p_r,
    pp_s, pp_r, sr_s, sl_s, sl_r, sr_r,
):
    pipe, tp = lax.axis_index("pipe"), lax.axis_index("tp")
    n_pipe = lax.axis_size("pipe")
    core = lax.rem(tp, 2)
    partner = tp + 1 - 2 * core
    right, left, opp = lax.rem(tp + 2, 8), lax.rem(tp + 6, 8), lax.rem(tp + 4, 8)
    chip = lax.div(tp, 2)
    nxt, prv = lax.rem(pipe + 1, n_pipe), lax.rem(pipe + n_pipe - 1, n_pipe)

    def rcopy(src, dst, send, recv, device):
        return pltpu.make_async_remote_copy(
            src_ref=src, dst_ref=dst, send_sem=send, recv_sem=recv, device_id=device, device_id_type=MESH
        )

    def landed(dst, recv):
        pltpu.make_async_copy(dst, dst, recv).wait()

    loads = [
        pltpu.make_async_copy(src, dst, ld_sem.at[i])
        for i, (src, dst) in enumerate(
            [
                (fkv, fkv_v), (fq, fq_v), (bkv, bkv_v), (bq, bq_v), (weight, w_v),
                (starts_h, starts),
            ]
        )
    ]
    barrier = pltpu.get_barrier_semaphore()
    peers = ((pipe, partner), (pipe, right), (pipe, left), (nxt, tp), (prv, tp))
    for peer in peers:
        pl.semaphore_signal(barrier, inc=1, device_id=peer, device_id_type=MESH)
    for load in (*loads[5:], *loads[:5]):
        load.start()
    for load in loads[5:]:
        load.wait()
    mic_out[...] = jnp.full(mic_out.shape, grad_micro[0], jnp.int32)

    first = [starts[0, d] for d in range(4)]
    for m in range(1, 4):
        first = [jnp.where(fwd_micro[0] == m, starts[m, d], first[d]) for d in range(4)]

    pl.semaphore_wait(barrier, len(peers))

    def rows_of(shard, k):
        return pl.ds(pl.multiple_of(shard * 64 + k * CROWS, CROWS), CROWS)

    def view(shard, p):
        chunk, first_col, cols = PIECES[p]
        return g_v.at[rows_of(shard, chunk), pl.ds(first_col, cols)]

    def z_copy(p):
        chunk, first_col, cols = PIECES[p]
        mine = grad.at[pl.ds(chunk * CROWS, CROWS), pl.ds(first_col, cols)]
        return rcopy(mine, view(tp, p), z_s.at[p], z_r.at[p], (prv, tp))

    mic = rcopy(mic_out, mic_in, mic_s, mic_r, (prv, tp))
    mic.start()
    for p in range(LAST):
        z_copy(p).start()

    last_rows = grad.at[pl.ds(3 * CROWS, CROWS), :]
    early_to_r = rcopy(last_rows, early_l, er_s, el_r, (pipe, right))
    early_to_l = rcopy(last_rows, early_r, el_s, er_r, (pipe, left))
    early_to_r.start()
    early_to_l.start()
    early_z_l = rcopy(early_l, view(left, LAST), ez_s.at[0], ez_r.at[0], (prv, tp))
    early_z_r = rcopy(early_r, view(right, LAST), ez_s.at[1], ez_r.at[1], (prv, tp))
    early_z_o = rcopy(early_o, view(opp, LAST), ez_s.at[2], ez_r.at[2], (prv, tp))
    half_a, half_b = pl.ds(0, HALF), pl.ds(HALF, HALF)
    onward_r = rcopy(early_l.at[:, half_a], early_o.at[:, half_a], eo_s.at[0], eo_r.at[0], (pipe, right))
    onward_l = rcopy(early_r.at[:, half_b], early_o.at[:, half_b], eo_s.at[1], eo_r.at[1], (pipe, left))

    loads[0].wait()
    loads[1].wait()

    def attn_copy(slot):
        return rcopy(attn_out.at[slot], attn_in.at[slot], at_s.at[slot], at_r.at[slot], (nxt, tp))

    @pl.loop(0, 4)
    def _(slot):
        row0 = pl.multiple_of(lax.rem(chip + slot + 2, 4) * 128, 128)
        row = lax.broadcasted_iota(jnp.int32, (128, R), 0) + row0
        column = lax.broadcasted_iota(jnp.int32, (128, R), 1)
        begin = jnp.zeros((128, R), jnp.int32)
        for d in range(4):
            begin = jnp.maximum(begin, jnp.where(row >= first[d], first[d], 0))
        bias = jnp.where((column >= begin) & (column <= row), 0.0, MASKED)
        for h in range(4):
            cols = slice(HD * h, HD * h + HD)
            scores = dot_nt(fq_v[pl.ds(row0, 128), cols], fkv_v[0]) + bias
            shifted = jnp.exp2((scores - jnp.max(scores, axis=1, keepdims=True)) * EXP_SCALE)
            total = jnp.sum(shifted, axis=1, keepdims=True)
            attn_out[slot, :, cols] = (dot(shifted.astype(BF16), fkv_v[1]) * (1.0 / total)).astype(BF16)
        attn_copy(slot).start()

    resid_copy = rcopy(resid, resid_in, rs_s, rs_r, (nxt, tp))
    resid_copy.start()
    loads[2].wait()
    loads[3].wait()
    mic.wait_recv()
    micro = mic_in[0:1, :]
    begins = []
    for d in range(4):
        value = jnp.zeros((1, 128), jnp.int32)
        for m in range(4):
            value = value + jnp.where(micro == m, starts[m, d], 0)
        begins.append(value)

    @pl.loop(0, 4)
    def _(block):
        col0 = pl.multiple_of(block * 128, 128)
        query = lax.broadcasted_iota(jnp.int32, (1, 128), 1) + col0
        begin = jnp.zeros((1, 128), jnp.int32)
        for d in range(4):
            begin = jnp.maximum(begin, jnp.where(query >= begins[d], begins[d], 0))
        key = lax.broadcasted_iota(jnp.int32, (R, 128), 0)
        bias_b[:, pl.ds(col0, 128)] = jnp.where((key >= begin) & (key <= query), 0.0, MASKED)

    kt_v[...] = bkv_v[0].astype(F32).T.astype(BF16)
    vt_v[...] = bkv_v[1].astype(F32).T.astype(BF16)
    dk_v[...] = jnp.zeros_like(dk_v)
    dv_v[...] = jnp.zeros_like(dv_v)

    def to_partner(kind, p, ref):
        return rcopy(ref, ref, p_s.at[kind, p], p_r.at[kind, p], (pipe, partner))

    def x_copies(p, with_chips=True):
        mine = view(tp, p)
        beside = (
            rcopy(mine, mine, xr_s.at[p], fl_r.at[p], (pipe, right)),
            rcopy(mine, mine, xl_s.at[p], fr_r.at[p], (pipe, left)),
        ) if with_chips else ()
        return (*beside, to_partner(0, p, mine))

    def left_copies(p):
        chunk = PIECES[p][0]
        theirs = g_v.at[rows_of(left, chunk), half_a]
        onward = (rcopy(theirs, theirs, yr_s.at[chunk], fl2_r.at[chunk], (pipe, right)),) if p not in (1, LAST) else ()
        return (*onward, to_partner(1, p, view(left, p)))

    def right_copies(p):
        chunk = PIECES[p][0]
        theirs = g_v.at[rows_of(right, chunk), half_b]
        onward = (rcopy(theirs, theirs, yl_s.at[chunk], fr2_r.at[chunk], (pipe, left)),) if p not in (0, LAST) else ()
        return (*onward, to_partner(2, p, view(right, p)))

    def opp_copy(k):
        return to_partner(3, k, g_v.at[rows_of(opp, k), :])

    def start_all(copies):
        for copy in copies:
            copy.start()

    def from_next(p):
        landed(view(tp, p), z_r.at[p])
        start_all(x_copies(p))

    def from_sides(p):
        landed(view(left, p), fl_r.at[p])
        start_all(left_copies(p))
        landed(view(right, p), fr_r.at[p])
        start_all(right_copies(p))

    def from_opp(k):
        landed(g_v.at[rows_of(opp, k), half_a], fl2_r.at[k])
        landed(g_v.at[rows_of(opp, k), half_b], fr2_r.at[k])
        opp_copy(k).start()

    def last_left():
        early_z_l.wait_recv()
        start_all(left_copies(LAST))

    def last_right():
        early_z_r.wait_recv()
        start_all(right_copies(LAST))

    def last_opp():
        early_z_o.wait_recv()
        opp_copy(CHUNKS - 1).start()

    def last_own():
        landed(view(tp, LAST), z_r.at[LAST])
        start_all(x_copies(LAST, False))

    @pl.loop(0, 4)
    def _(h):
        @pl.when(h == 0)
        def _():
            from_next(0)

        @pl.when(h == 1)
        def _():
            early_to_r.wait_recv()
            onward_r.start()
            early_z_l.start()
            early_to_l.wait_recv()
            onward_l.start()
            early_z_r.start()
            z_copy(LAST).start()

        @pl.when(h == 2)
        def _():
            from_next(1)

        cols = pl.ds(pl.multiple_of(h * HD, HD), HD)
        for b in range(2):
            n = 256 * (b + 1)
            rows = slice(256 * b, n)
            scores = dot_nt(bkv_v[0, :n, :], bq_v[rows, cols]) + bias_b[:n, rows]
            shifted = jnp.exp2((scores - jnp.max(scores, axis=0, keepdims=True)) * EXP_SCALE)
            total = jnp.sum(shifted, axis=0, keepdims=True)
            probs = (shifted * (1.0 / total)).astype(BF16)
            pt_v[h, :n, rows] = probs
            bat_v[cols, rows] = dot(vt_v[:, :n], probs).astype(BF16)

    from_next(2)
    from_sides(0)
    from_sides(1)
    from_next(3)

    loads[4].wait()

    def project(pair, half):
        lhs = jnp.concatenate([attn_in[slot] for slot in pair], axis=0)

        @pl.loop(4 * half, 4 * half + 4)
        def _(tile):
            cols = pl.ds(pl.multiple_of(tile * TILE, TILE), TILE)
            product = dot(lhs, w_v[:, cols]).astype(BF16)
            for i, slot in enumerate(pair):
                for c in range(2):
                    part[slot, c, :, cols] = product[128 * i + 64 * c : 128 * i + 64 * c + 64, :]

        for slot in pair:
            pp_copy(slot, half).start()

    halves = (half_a, half_b)

    def pp_copy(slot, half):
        return rcopy(
            part.at[slot, 1 - core, :, halves[half]], recvp.at[slot, :, halves[half]],
            pp_s.at[slot, half], pp_r.at[slot, half], (pipe, partner),
        )

    def chip_sum(slot, half, cols):
        begin = half * HALF + cols
        window = pl.ds(pl.multiple_of(begin, TILE), TILE)
        return part[slot, core, :, window].astype(F32) + recvp[slot, :, window].astype(F32)

    def opp_half(half):
        landed(recvp.at[OPP, :, halves[half]], pp_r.at[OPP, half])

        @pl.loop(0, HALF, step=TILE)
        def _(cols):
            opp_sum[half, :, pl.ds(pl.multiple_of(cols, TILE), TILE)] = chip_sum(OPP, half, cols).astype(BF16)

    send_opp_r = rcopy(opp_sum.at[0], rel_l, sr_s.at[0], sl_r.at[0], (pipe, right))
    send_opp_l = rcopy(opp_sum.at[1], rel_r, sl_s.at[0], sr_r.at[0], (pipe, left))
    send_side_l = rcopy(side_sum.at[0], fin_r.at[0], sl_s.at[1], sr_r.at[1], (pipe, left))
    send_side_r = rcopy(side_sum.at[1], fin_l.at[1], sr_s.at[1], sl_r.at[1], (pipe, right))
    send_acc_r = rcopy(acc_r, fin_l.at[0], sr_s.at[2], sl_r.at[2], (pipe, right))
    send_acc_l = rcopy(acc_l, fin_r.at[1], sl_s.at[2], sr_r.at[2], (pipe, left))

    def side_half(slot, half):
        landed(recvp.at[slot, :, halves[half]], pp_r.at[slot, half])

        @pl.loop(0, HALF, step=TILE)
        def _(cols):
            side_sum[half, :, pl.ds(pl.multiple_of(cols, TILE), TILE)] = chip_sum(slot, half, cols).astype(BF16)

    def landed_attn(pair):
        for slot in pair:
            landed(attn_in.at[slot], at_r.at[slot])

    near, far = (OWN, RIGHT), (OPP, LEFT)
    landed_attn(far)
    project(far, 0)
    onward_r.wait_recv()
    onward_l.wait_recv()
    early_z_o.start()
    project(far, 1)
    from_sides(2)
    from_opp(0)
    opp_half(0)
    opp_half(1)
    last_left()
    landed_attn(near)
    project(near, 0)
    from_sides(3)
    send_opp_r.start()
    project(near, 1)
    last_right()
    send_opp_l.start()
    side_half(LEFT, 0)
    send_side_l.start()
    from_opp(1)

    peer_shards = [lax.rem(shard, 8) + 1 - 2 * core for shard in (tp, left, right, opp)]

    def attn_grad(half):
        for k in (2 * half, 2 * half + 1):
            for kind, shard in enumerate(peer_shards[:3]):
                for p in range(len(PIECES)):
                    if PIECES[p][0] == k:
                        landed(view(shard, p), p_r.at[kind, p])
            landed(g_v.at[rows_of(peer_shards[3], k), :], p_r.at[3, k])
        acc_v[...] = jnp.zeros_like(acc_v)

        @pl.loop(0, D // DEEP)
        def _(tile):
            cols = pl.ds(pl.multiple_of(tile * DEEP, DEEP), DEEP)
            lhs = jnp.concatenate([g_v[64 * i + 32 * half : 64 * i + 32 * half + 32, cols] for i in range(8)], axis=0)
            acc_v[...] += dot_nt(lhs, w_v[:, cols])

        for i in range(8):
            ga_v[64 * i + 32 * half : 64 * i + 32 * half + 32, :] = acc_v[32 * i : 32 * i + 32, :].astype(BF16)


    @pl.when(core == 1)
    def _():
        from_opp(2)
        last_own()

    side_half(RIGHT, 1)
    send_side_r.start()
    attn_grad(0)

    @pl.when(core == 0)
    def _():
        last_own()
        from_opp(2)

    last_opp()
    attn_grad(1)

    def gw_copy(tile):
        cols = pl.ds(pl.multiple_of(tile * TILE, TILE), TILE)
        return pltpu.make_async_copy(gw_v.at[:, cols], gw.at[:, cols], gw_sem.at[tile])

    def weight_grad(first_tile, stop):
        @pl.loop(first_tile, stop)
        def _(tile):
            cols = pl.ds(pl.multiple_of(tile * TILE, TILE), TILE)
            gw_v[:, cols] = dot(bat_v[...], g_v[:, cols]).astype(BF16)
            gw_copy(tile).start()

    weight_grad(0, 4)

    landed(rel_l, sl_r.at[0])
    landed(recvp.at[RIGHT, :, half_a], pp_r.at[RIGHT, 0])
    landed(rel_r, sr_r.at[0])
    landed(recvp.at[LEFT, :, half_b], pp_r.at[LEFT, 1])

    @pl.loop(0, HALF, step=TILE)
    def _(cols):
        window = pl.ds(pl.multiple_of(cols, TILE), TILE)
        acc_r[:, window] = (chip_sum(RIGHT, 0, cols) + rel_l[:, window].astype(F32)).astype(BF16)
        acc_l[:, window] = (chip_sum(LEFT, 1, cols) + rel_r[:, window].astype(F32)).astype(BF16)

    send_acc_r.start()
    send_acc_l.start()

    weight_grad(4, D // TILE)

    @pl.loop(0, 4)
    def _(h):
        cols = pl.ds(pl.multiple_of(h * HD, HD), HD)
        for b in range(2):
            n = 256 * (b + 1)
            rows = slice(256 * b, n)
            grad_rows = ga_v[rows, cols]
            dprob = dot_nt(bkv_v[1, :n, :], grad_rows)
            probs = pt_v[h, :n, rows]
            wide = probs.astype(F32)
            delta = jnp.sum(wide * dprob, axis=0, keepdims=True)
            dscore = (wide * (dprob - delta) * SCALE).astype(BF16)
            gq_v[rows, cols] = dot(kt_v[:, :n], dscore).T.astype(BF16)
            dk_v[:n, :] += dot(dscore, bq_v[rows, cols])
            dv_v[:n, :] += dot(probs, grad_rows)

    gkv_v[0] = dk_v[...].astype(BF16)
    gkv_v[1] = dv_v[...].astype(BF16)
    stores = [pltpu.make_async_copy(gq_v, gq, st_sem.at[0]), pltpu.make_async_copy(gkv_v, gkv, st_sem.at[1])]
    for store in stores:
        store.start()

    resid_copy.wait_recv()
    for half in range(2):
        landed(recvp.at[OWN, :, halves[half]], pp_r.at[OWN, half])

        @pl.loop(0, HALF, step=TILE)
        def _(cols):
            place = pl.ds(pl.multiple_of(half * HALF + cols, TILE), TILE)
            base_v[:, place] = resid_in[:, place].astype(F32) + chip_sum(OWN, half, cols)

    store = pltpu.make_async_copy(base_v, base, st_sem.at[2])
    store.start()
    stores.append(store)
    for half in range(2):
        landed(fin_l.at[half], sl_r.at[2 if half == 0 else 1])
        landed(fin_r.at[half], sr_r.at[1 if half == 0 else 2])

    mic.wait_send()
    resid_copy.wait_send()
    for h in range(4):
        attn_copy(h).wait_send()
    for copy in (early_to_r, early_to_l, onward_r, onward_l, early_z_l, early_z_r, early_z_o):
        copy.wait_send()
    for p in range(len(PIECES)):
        for copy in (z_copy(p), *x_copies(p, p < LAST), *left_copies(p), *right_copies(p)):
            copy.wait_send()
    for k in range(CHUNKS):
        opp_copy(k).wait_send()
    for slot in range(4):
        for half in range(2):
            pp_copy(slot, half).wait_send()
    for copy in (send_opp_r, send_opp_l, send_side_l, send_side_r, send_acc_r, send_acc_l):
        copy.wait_send()
    for tile in range(D // TILE):
        gw_copy(tile).wait()
    for store in stores:
        store.wait()


def deliver(
    gw, gq, gkv, base, fin_l, fin_r, gw_out, gq_out, gkv_out, out,
    base_v, left_v, right_v, out_v, sem, in_sem, out_sem,
):
    sides = [
        pltpu.make_async_copy(src, dst, in_sem.at[i])
        for i, (src, dst) in enumerate([(base, base_v), (fin_l, left_v), (fin_r, right_v)])
    ]
    pieces = []
    for src, dst in ((gw, gw_out), (gq, gq_out), (gkv, gkv_out)):
        for lead in range(src.shape[0]):
            for row in range(0, src.shape[1], 64):
                pieces.append(tuple(ref.at[lead, pl.ds(row, 64), :] for ref in (src, dst)))
    copies = [pltpu.make_async_copy(a, b, sem.at[i]) for i, (a, b) in enumerate(pieces)]
    for copy in (*sides, *copies):
        copy.start()
    for side in sides:
        side.wait()
    for half in range(2):

        @pl.loop(0, HALF, step=TILE)
        def _(cols):
            window = pl.ds(pl.multiple_of(cols, TILE), TILE)
            place = pl.ds(pl.multiple_of(half * HALF + cols, TILE), TILE)
            total = base_v[:, place] + left_v[half, :, window].astype(F32) + right_v[half, :, window].astype(F32)
            out_v[:, place] = total.astype(BF16)

        columns = pl.ds(half * HALF, HALF)
        copies.append(pltpu.make_async_copy(out_v.at[:, columns], out.at[0, :, columns], out_sem.at[half]))
        copies[-1].start()
    for copy in copies:
        copy.wait()


def shards(fwd_resid, fwd_query, fwd_keyval, fwd_micro, bwd_query, bwd_keyval, grad_micro, grad_in, out_weight, doc_starts):
    any_space = pl.BlockSpec(memory_space=pl.ANY)
    smem = pl.BlockSpec(memory_space=pltpu.SMEM)
    dma = pltpu.SemaphoreType.DMA
    vmem = pltpu.VMEM
    scratch = [
        pltpu.SMEM((4, 4), jnp.int32),
        vmem((R, R), BF16), vmem((2, R, HD), BF16), vmem((R, R), BF16), vmem((2, R, HD), BF16),
        vmem((R, D), BF16), vmem((R, D), BF16),
        vmem((4, HD, R), BF16), vmem((4, HD, R), BF16), vmem((64, D), BF16),
        vmem((8, 128), jnp.int32), vmem((8, 128), jnp.int32),
        vmem((R, R), F32), vmem((HD, R), BF16), vmem((HD, R), BF16),
        vmem((4, R, R), BF16), vmem((R, R), BF16), vmem((R // 2, R), F32), vmem((R, R), BF16),
        vmem((R, HD), F32), vmem((R, HD), F32), vmem((R, R), BF16), vmem((2, R, HD), BF16), vmem((R, D), BF16),
        vmem((4, 2, 64, D), BF16), vmem((4, 64, D), BF16), vmem((2, 64, HALF), BF16), vmem((2, 64, HALF), BF16),
        vmem((64, HALF), BF16), vmem((64, HALF), BF16),
        vmem((64, HALF), BF16), vmem((64, HALF), BF16), vmem((64, D), F32),
        dma((6,)), dma((4,)), dma((D // TILE,)),
        vmem((CROWS, D), BF16), vmem((CROWS, D), BF16), vmem((CROWS, D), BF16),
        dma, dma, dma, dma, dma((2,)), dma((2,)), dma((3,)), dma((3,)),
        dma((len(PIECES),)), dma((len(PIECES),)), dma, dma, dma((4,)), dma((4,)), dma, dma,
        dma((LAST,)), dma((LAST,)), dma((LAST,)), dma((LAST,)),
        dma((CHUNKS,)), dma((CHUNKS,)), dma((CHUNKS,)), dma((CHUNKS,)),
        dma((4, len(PIECES))), dma((4, len(PIECES))),
        dma((4, 2)), dma((4, 2)), dma((3,)), dma((3,)), dma((3,)), dma((3,)),
    ]
    base, gq, gkv, gw, fin_l, fin_r = pl.pallas_call(
        kernel,
        out_shape=(
            jax.ShapeDtypeStruct((64, D), F32),
            jax.ShapeDtypeStruct((R, R), BF16),
            jax.ShapeDtypeStruct((2, R, HD), BF16),
            jax.ShapeDtypeStruct((R, D), BF16),
            jax.ShapeDtypeStruct((2, 64, HALF), BF16),
            jax.ShapeDtypeStruct((2, 64, HALF), BF16),
        ),
        in_specs=[smem] * 2 + [pl.BlockSpec(memory_space=pltpu.HBM)] * 8,
        out_specs=(any_space,) * 6,
        scratch_shapes=scratch,
        compiler_params=pltpu.CompilerParams(
            collective_id=0, has_side_effects=True, vmem_limit_bytes=40 * 1024 * 1024
        ),
    )(
        fwd_micro, grad_micro, pltpu.with_memory_space_constraint(doc_starts, pltpu.HBM),
        *(
            pltpu.with_memory_space_constraint(a[0], pltpu.HBM)
            for a in (fwd_resid, fwd_query, fwd_keyval, bwd_query, bwd_keyval, grad_in, out_weight)
        ),
    )
    arrays = (gw[None], gq[None], gkv)
    count = sum(a.shape[0] * (a.shape[1] // 64) for a in arrays)
    gw, gq, gkv, out = pl.pallas_call(
        deliver,
        out_shape=(
            *(jax.ShapeDtypeStruct(a.shape, a.dtype) for a in arrays),
            jax.ShapeDtypeStruct((1, 64, D), BF16),
        ),
        in_specs=[any_space] * 6,
        out_specs=(any_space,) * 4,
        scratch_shapes=[
            vmem((64, D), F32), vmem((2, 64, HALF), BF16), vmem((2, 64, HALF), BF16), vmem((64, D), BF16),
            dma((count,)), dma((3,)), dma((2,)),
        ],
        compiler_params=pltpu.CompilerParams(vmem_limit_bytes=8 * 1024 * 1024),
    )(*arrays, base, fin_l, fin_r)
    return (out, gq, gkv[None], gw)


def solution(mesh):
    return jax.shard_map(
        shards,
        mesh=mesh,
        in_specs=(
            P("pipe", "tp", None),
            P("pipe", None, "tp"),
            P("pipe", None, None, "tp"),
            P("pipe"),
            P("pipe", None, "tp"),
            P("pipe", None, None, "tp"),
            P("pipe"),
            P("pipe", "tp", None),
            P("pipe", "tp", None),
            P(),
        ),
        out_specs=(
            P("pipe", "tp", None),
            P("pipe", None, "tp"),
            P("pipe", None, None, "tp"),
            P("pipe", "tp", None),
        ),
        check_vma=False,
    )
```

```python
import functools
import math

import jax
import jax.numpy as jnp
from jax import lax
from jax.experimental import pallas as pl
from jax.experimental.pallas import tpu as pltpu
from jax.sharding import PartitionSpec as P

MESH = pl.DeviceIdType.MESH
F32 = jnp.float32
BF16 = jnp.bfloat16
R = 512
D = 4096
HD = 128
HALF = D // 2
SCALE = 1.0 / math.sqrt(HD)
EXP_SCALE = SCALE * math.log2(math.e)
MASKED = -1e30
CHUNKS = 4
CROWS = 64 // CHUNKS
TILE = 512
DEEP = 1024
PIECES = ((0, 0, HALF), (0, HALF, HALF), (1, 0, D), (2, 0, D), (3, 0, D))
LAST = len(PIECES) - 1
OPP, LEFT, OWN, RIGHT = 0, 1, 2, 3


def dot(a, b):
    return jnp.dot(a, b, preferred_element_type=F32)


def dot_nt(a, b):
    return lax.dot_general(a, b, (((1,), (1,)), ((), ())), preferred_element_type=F32)


def kernel(
    fwd_micro, grad_micro, starts_h, resid, fq, fkv, bq, bkv, grad, weight,
    base, gq, gkv, gw, fin_l, fin_r,
    starts, fq_v, fkv_v, bq_v, bkv_v, w_v, g_v, attn_out, attn_in, resid_in, mic_out, mic_in,
    bias_b, kt_v, vt_v, pt_v, bat_v, acc_v, ga_v, dk_v, dv_v, gq_v, gkv_v, gw_v,
    part, recvp, opp_sum, side_sum, rel_l, rel_r, acc_r, acc_l, base_v,
    ld_sem, st_sem, gw_sem,
    early_l, early_r, early_o, el_s, el_r, er_s, er_r, eo_s, eo_r, ez_s, ez_r,
    z_s, z_r, mic_s, mic_r, at_s, at_r, rs_s, rs_r,
    xr_s, xl_s, fl_r, fr_r, yr_s, yl_s, fl2_r, fr2_r, p_s, p_r,
    pp_s, pp_r, sr_s, sl_s, sl_r, sr_r,
):
    pipe, tp = lax.axis_index("pipe"), lax.axis_index("tp")
    n_pipe = lax.axis_size("pipe")
    core = lax.rem(tp, 2)
    partner = tp + 1 - 2 * core
    right, left, opp = lax.rem(tp + 2, 8), lax.rem(tp + 6, 8), lax.rem(tp + 4, 8)
    chip = lax.div(tp, 2)
    nxt, prv = lax.rem(pipe + 1, n_pipe), lax.rem(pipe + n_pipe - 1, n_pipe)

    def rcopy(src, dst, send, recv, device):
        return pltpu.make_async_remote_copy(
            src_ref=src, dst_ref=dst, send_sem=send, recv_sem=recv, device_id=device, device_id_type=MESH
        )

    def landed(dst, recv):
        pltpu.make_async_copy(dst, dst, recv).wait()

    loads = [
        pltpu.make_async_copy(src, dst, ld_sem.at[i])
        for i, (src, dst) in enumerate(
            [
                (fkv, fkv_v), (fq, fq_v), (bkv, bkv_v), (bq, bq_v), (weight, w_v),
                (starts_h, starts),
            ]
        )
    ]
    barrier = pltpu.get_barrier_semaphore()
    peers = ((pipe, partner), (pipe, right), (pipe, left), (nxt, tp), (prv, tp))
    for peer in peers:
        pl.semaphore_signal(barrier, inc=1, device_id=peer, device_id_type=MESH)
    for load in (*loads[5:], *loads[:5]):
        load.start()
    for load in loads[5:]:
        load.wait()
    mic_out[...] = jnp.full(mic_out.shape, grad_micro[0], jnp.int32)

    first = [starts[0, d] for d in range(4)]
    for m in range(1, 4):
        first = [jnp.where(fwd_micro[0] == m, starts[m, d], first[d]) for d in range(4)]

    pl.semaphore_wait(barrier, len(peers))

    def rows_of(shard, k):
        return pl.ds(pl.multiple_of(shard * 64 + k * CROWS, CROWS), CROWS)

    def view(shard, p):
        chunk, first_col, cols = PIECES[p]
        return g_v.at[rows_of(shard, chunk), pl.ds(first_col, cols)]

    def z_copy(p):
        chunk, first_col, cols = PIECES[p]
        mine = grad.at[pl.ds(chunk * CROWS, CROWS), pl.ds(first_col, cols)]
        return rcopy(mine, view(tp, p), z_s.at[p], z_r.at[p], (prv, tp))

    mic = rcopy(mic_out, mic_in, mic_s, mic_r, (prv, tp))
    mic.start()
    for p in range(LAST):
        z_copy(p).start()

    last_rows = grad.at[pl.ds(3 * CROWS, CROWS), :]
    early_to_r = rcopy(last_rows, early_l, er_s, el_r, (pipe, right))
    early_to_l = rcopy(last_rows, early_r, el_s, er_r, (pipe, left))
    early_to_r.start()
    early_to_l.start()
    early_z_l = rcopy(early_l, view(left, LAST), ez_s.at[0], ez_r.at[0], (prv, tp))
    early_z_r = rcopy(early_r, view(right, LAST), ez_s.at[1], ez_r.at[1], (prv, tp))
    early_z_o = rcopy(early_o, view(opp, LAST), ez_s.at[2], ez_r.at[2], (prv, tp))
    half_a, half_b = pl.ds(0, HALF), pl.ds(HALF, HALF)
    onward_r = rcopy(early_l.at[:, half_a], early_o.at[:, half_a], eo_s.at[0], eo_r.at[0], (pipe, right))
    onward_l = rcopy(early_r.at[:, half_b], early_o.at[:, half_b], eo_s.at[1], eo_r.at[1], (pipe, left))

    loads[0].wait()
    loads[1].wait()

    def attn_copy(slot):
        return rcopy(attn_out.at[slot], attn_in.at[slot], at_s.at[slot], at_r.at[slot], (nxt, tp))

    @pl.loop(0, 4)
    def _(slot):
        row0 = pl.multiple_of(lax.rem(chip + slot + 2, 4) * 128, 128)
        row = lax.broadcasted_iota(jnp.int32, (128, R), 0) + row0
        column = lax.broadcasted_iota(jnp.int32, (128, R), 1)
        begin = jnp.zeros((128, R), jnp.int32)
        for d in range(4):
            begin = jnp.maximum(begin, jnp.where(row >= first[d], first[d], 0))
        bias = jnp.where((column >= begin) & (column <= row), 0.0, MASKED)
        for h in range(4):
            cols = slice(HD * h, HD * h + HD)
            scores = dot_nt(fq_v[pl.ds(row0, 128), cols], fkv_v[0]) + bias
            shifted = jnp.exp2((scores - jnp.max(scores, axis=1, keepdims=True)) * EXP_SCALE)
            total = jnp.sum(shifted, axis=1, keepdims=True)
            attn_out[slot, :, cols] = (dot(shifted.astype(BF16), fkv_v[1]) * (1.0 / total)).astype(BF16)
        attn_copy(slot).start()

    resid_copy = rcopy(resid, resid_in, rs_s, rs_r, (nxt, tp))
    resid_copy.start()
    loads[2].wait()
    loads[3].wait()
    mic.wait_recv()
    micro = mic_in[0:1, :]
    begins = []
    for d in range(4):
        value = jnp.zeros((1, 128), jnp.int32)
        for m in range(4):
            value = value + jnp.where(micro == m, starts[m, d], 0)
        begins.append(value)

    @pl.loop(0, 4)
    def _(block):
        col0 = pl.multiple_of(block * 128, 128)
        query = lax.broadcasted_iota(jnp.int32, (1, 128), 1) + col0
        begin = jnp.zeros((1, 128), jnp.int32)
        for d in range(4):
            begin = jnp.maximum(begin, jnp.where(query >= begins[d], begins[d], 0))
        key = lax.broadcasted_iota(jnp.int32, (R, 128), 0)
        bias_b[:, pl.ds(col0, 128)] = jnp.where((key >= begin) & (key <= query), 0.0, MASKED)

    kt_v[...] = bkv_v[0].astype(F32).T.astype(BF16)
    vt_v[...] = bkv_v[1].astype(F32).T.astype(BF16)
    dk_v[...] = jnp.zeros_like(dk_v)
    dv_v[...] = jnp.zeros_like(dv_v)

    def to_partner(kind, p, ref):
        return rcopy(ref, ref, p_s.at[kind, p], p_r.at[kind, p], (pipe, partner))

    def x_copies(p, with_chips=True):
        mine = view(tp, p)
        beside = (
            rcopy(mine, mine, xr_s.at[p], fl_r.at[p], (pipe, right)),
            rcopy(mine, mine, xl_s.at[p], fr_r.at[p], (pipe, left)),
        ) if with_chips else ()
        return (*beside, to_partner(0, p, mine))

    def left_copies(p):
        chunk = PIECES[p][0]
        theirs = g_v.at[rows_of(left, chunk), half_a]
        onward = (rcopy(theirs, theirs, yr_s.at[chunk], fl2_r.at[chunk], (pipe, right)),) if p not in (1, LAST) else ()
        return (*onward, to_partner(1, p, view(left, p)))

    def right_copies(p):
        chunk = PIECES[p][0]
        theirs = g_v.at[rows_of(right, chunk), half_b]
        onward = (rcopy(theirs, theirs, yl_s.at[chunk], fr2_r.at[chunk], (pipe, left)),) if p not in (0, LAST) else ()
        return (*onward, to_partner(2, p, view(right, p)))

    def opp_copy(k):
        return to_partner(3, k, g_v.at[rows_of(opp, k), :])

    def start_all(copies):
        for copy in copies:
            copy.start()

    def from_next(p):
        landed(view(tp, p), z_r.at[p])
        start_all(x_copies(p))

    def from_sides(p):
        landed(view(left, p), fl_r.at[p])
        start_all(left_copies(p))
        landed(view(right, p), fr_r.at[p])
        start_all(right_copies(p))

    def from_opp(k):
        landed(g_v.at[rows_of(opp, k), half_a], fl2_r.at[k])
        landed(g_v.at[rows_of(opp, k), half_b], fr2_r.at[k])
        opp_copy(k).start()

    def last_left():
        early_z_l.wait_recv()
        start_all(left_copies(LAST))

    def last_right():
        early_z_r.wait_recv()
        start_all(right_copies(LAST))

    def last_opp():
        early_z_o.wait_recv()
        opp_copy(CHUNKS - 1).start()

    def last_own():
        landed(view(tp, LAST), z_r.at[LAST])
        start_all(x_copies(LAST, False))

    @pl.loop(0, 4)
    def _(h):
        @pl.when(h == 0)
        def _():
            from_next(0)

        @pl.when(h == 1)
        def _():
            early_to_r.wait_recv()
            onward_r.start()
            early_z_l.start()
            early_to_l.wait_recv()
            onward_l.start()
            early_z_r.start()
            z_copy(LAST).start()

        @pl.when(h == 2)
        def _():
            from_next(1)

        cols = pl.ds(pl.multiple_of(h * HD, HD), HD)
        for b in range(2):
            n = 256 * (b + 1)
            rows = slice(256 * b, n)
            scores = dot_nt(bkv_v[0, :n, :], bq_v[rows, cols]) + bias_b[:n, rows]
            shifted = jnp.exp2((scores - jnp.max(scores, axis=0, keepdims=True)) * EXP_SCALE)
            total = jnp.sum(shifted, axis=0, keepdims=True)
            probs = (shifted * (1.0 / total)).astype(BF16)
            pt_v[h, :n, rows] = probs
            bat_v[cols, rows] = dot(vt_v[:, :n], probs).astype(BF16)

    from_next(2)
    from_sides(0)
    from_sides(1)
    from_next(3)

    loads[4].wait()

    def project(pair, half):
        lhs = jnp.concatenate([attn_in[slot] for slot in pair], axis=0)

        @pl.loop(4 * half, 4 * half + 4)
        def _(tile):
            cols = pl.ds(pl.multiple_of(tile * TILE, TILE), TILE)
            product = dot(lhs, w_v[:, cols]).astype(BF16)
            for i, slot in enumerate(pair):
                for c in range(2):
                    part[slot, c, :, cols] = product[128 * i + 64 * c : 128 * i + 64 * c + 64, :]

        for slot in pair:
            pp_copy(slot, half).start()

    halves = (half_a, half_b)

    def pp_copy(slot, half):
        return rcopy(
            part.at[slot, 1 - core, :, halves[half]], recvp.at[slot, :, halves[half]],
            pp_s.at[slot, half], pp_r.at[slot, half], (pipe, partner),
        )

    def chip_sum(slot, half, cols):
        begin = half * HALF + cols
        window = pl.ds(pl.multiple_of(begin, TILE), TILE)
        return part[slot, core, :, window].astype(F32) + recvp[slot, :, window].astype(F32)

    def opp_half(half):
        landed(recvp.at[OPP, :, halves[half]], pp_r.at[OPP, half])

        @pl.loop(0, HALF, step=TILE)
        def _(cols):
            opp_sum[half, :, pl.ds(pl.multiple_of(cols, TILE), TILE)] = chip_sum(OPP, half, cols).astype(BF16)

    send_opp_r = rcopy(opp_sum.at[0], rel_l, sr_s.at[0], sl_r.at[0], (pipe, right))
    send_opp_l = rcopy(opp_sum.at[1], rel_r, sl_s.at[0], sr_r.at[0], (pipe, left))
    send_side_l = rcopy(side_sum.at[0], fin_r.at[0], sl_s.at[1], sr_r.at[1], (pipe, left))
    send_side_r = rcopy(side_sum.at[1], fin_l.at[1], sr_s.at[1], sl_r.at[1], (pipe, right))
    send_acc_r = rcopy(acc_r, fin_l.at[0], sr_s.at[2], sl_r.at[2], (pipe, right))
    send_acc_l = rcopy(acc_l, fin_r.at[1], sl_s.at[2], sr_r.at[2], (pipe, left))

    def side_half(slot, half):
        landed(recvp.at[slot, :, halves[half]], pp_r.at[slot, half])

        @pl.loop(0, HALF, step=TILE)
        def _(cols):
            side_sum[half, :, pl.ds(pl.multiple_of(cols, TILE), TILE)] = chip_sum(slot, half, cols).astype(BF16)

    def landed_attn(pair):
        for slot in pair:
            landed(attn_in.at[slot], at_r.at[slot])

    near, far = (OWN, RIGHT), (OPP, LEFT)
    landed_attn(far)
    project(far, 0)
    onward_r.wait_recv()
    onward_l.wait_recv()
    early_z_o.start()
    project(far, 1)
    from_sides(2)
    from_opp(0)
    opp_half(0)
    opp_half(1)
    last_left()
    landed_attn(near)
    project(near, 0)
    from_sides(3)
    send_opp_r.start()
    project(near, 1)
    last_right()
    send_opp_l.start()
    side_half(LEFT, 0)
    send_side_l.start()
    from_opp(1)

    peer_shards = [lax.rem(shard, 8) + 1 - 2 * core for shard in (tp, left, right, opp)]

    def attn_grad(half):
        for k in (2 * half, 2 * half + 1):
            for kind, shard in enumerate(peer_shards[:3]):
                for p in range(len(PIECES)):
                    if PIECES[p][0] == k:
                        landed(view(shard, p), p_r.at[kind, p])
            landed(g_v.at[rows_of(peer_shards[3], k), :], p_r.at[3, k])
        acc_v[...] = jnp.zeros_like(acc_v)

        @pl.loop(0, D // DEEP)
        def _(tile):
            cols = pl.ds(pl.multiple_of(tile * DEEP, DEEP), DEEP)
            lhs = jnp.concatenate([g_v[64 * i + 32 * half : 64 * i + 32 * half + 32, cols] for i in range(8)], axis=0)
            acc_v[...] += dot_nt(lhs, w_v[:, cols])

        for i in range(8):
            ga_v[64 * i + 32 * half : 64 * i + 32 * half + 32, :] = acc_v[32 * i : 32 * i + 32, :].astype(BF16)


    @pl.when(core == 1)
    def _():
        from_opp(2)
        last_own()

    side_half(RIGHT, 1)
    send_side_r.start()
    attn_grad(0)

    @pl.when(core == 0)
    def _():
        last_own()
        from_opp(2)

    last_opp()
    attn_grad(1)

    def gw_copy(tile):
        cols = pl.ds(pl.multiple_of(tile * TILE, TILE), TILE)
        return pltpu.make_async_copy(gw_v.at[:, cols], gw.at[:, cols], gw_sem.at[tile])

    def weight_grad(first_tile, stop):
        @pl.loop(first_tile, stop)
        def _(tile):
            cols = pl.ds(pl.multiple_of(tile * TILE, TILE), TILE)
            gw_v[:, cols] = dot(bat_v[...], g_v[:, cols]).astype(BF16)
            gw_copy(tile).start()

    weight_grad(0, 3)

    def running_sum(slot, half, arrived, arrival, result):
        landed(arrived, arrival)
        landed(recvp.at[slot, :, halves[half]], pp_r.at[slot, half])

        @pl.loop(0, HALF, step=TILE)
        def _(cols):
            window = pl.ds(pl.multiple_of(cols, TILE), TILE)
            result[:, window] = (chip_sum(slot, half, cols) + arrived[:, window].astype(F32)).astype(BF16)

    running_sum(RIGHT, 0, rel_l, sl_r.at[0], acc_r)
    send_acc_r.start()
    running_sum(LEFT, 1, rel_r, sr_r.at[0], acc_l)
    send_acc_l.start()
    weight_grad(3, D // TILE)

    @pl.loop(0, 4)
    def _(h):
        cols = pl.ds(pl.multiple_of(h * HD, HD), HD)
        for b in range(2):
            n = 256 * (b + 1)
            rows = slice(256 * b, n)
            grad_rows = ga_v[rows, cols]
            dprob = dot_nt(bkv_v[1, :n, :], grad_rows)
            probs = pt_v[h, :n, rows]
            wide = probs.astype(F32)
            delta = jnp.sum(wide * dprob, axis=0, keepdims=True)
            dscore = (wide * (dprob - delta) * SCALE).astype(BF16)
            gq_v[rows, cols] = dot(kt_v[:, :n], dscore).T.astype(BF16)
            dk_v[:n, :] += dot(dscore, bq_v[rows, cols])
            dv_v[:n, :] += dot(probs, grad_rows)

    gkv_v[0] = dk_v[...].astype(BF16)
    gkv_v[1] = dv_v[...].astype(BF16)
    stores = [pltpu.make_async_copy(gq_v, gq, st_sem.at[0]), pltpu.make_async_copy(gkv_v, gkv, st_sem.at[1])]
    for store in stores:
        store.start()

    resid_copy.wait_recv()
    for half in range(2):
        landed(recvp.at[OWN, :, halves[half]], pp_r.at[OWN, half])

        @pl.loop(0, HALF, step=TILE)
        def _(cols):
            place = pl.ds(pl.multiple_of(half * HALF + cols, TILE), TILE)
            base_v[:, place] = resid_in[:, place].astype(F32) + chip_sum(OWN, half, cols)

    store = pltpu.make_async_copy(base_v, base, st_sem.at[2])
    store.start()
    stores.append(store)
    for half in range(2):
        landed(fin_l.at[half], sl_r.at[2 if half == 0 else 1])
        landed(fin_r.at[half], sr_r.at[1 if half == 0 else 2])

    mic.wait_send()
    resid_copy.wait_send()
    for h in range(4):
        attn_copy(h).wait_send()
    for copy in (early_to_r, early_to_l, onward_r, onward_l, early_z_l, early_z_r, early_z_o):
        copy.wait_send()
    for p in range(len(PIECES)):
        for copy in (z_copy(p), *x_copies(p, p < LAST), *left_copies(p), *right_copies(p)):
            copy.wait_send()
    for k in range(CHUNKS):
        opp_copy(k).wait_send()
    for slot in range(4):
        for half in range(2):
            pp_copy(slot, half).wait_send()
    for copy in (send_opp_r, send_opp_l, send_side_l, send_side_r, send_acc_r, send_acc_l):
        copy.wait_send()
    for tile in range(D // TILE):
        gw_copy(tile).wait()
    for store in stores:
        store.wait()


def deliver(
    gw, gq, gkv, base, fin_l, fin_r, gw_out, gq_out, gkv_out, out,
    base_v, left_v, right_v, out_v, sem, in_sem, out_sem,
):
    sides = [
        pltpu.make_async_copy(src, dst, in_sem.at[i])
        for i, (src, dst) in enumerate([(base, base_v), (fin_l, left_v), (fin_r, right_v)])
    ]
    pieces = []
    for src, dst in ((gw, gw_out), (gq, gq_out), (gkv, gkv_out)):
        for lead in range(src.shape[0]):
            step = 64 if src.shape[2] == D else src.shape[1]
            for row in range(0, src.shape[1], step):
                pieces.append(tuple(ref.at[lead, pl.ds(row, step), :] for ref in (src, dst)))
    copies = [pltpu.make_async_copy(a, b, sem.at[i]) for i, (a, b) in enumerate(pieces)]
    for copy in (*sides, *copies):
        copy.start()
    for side in sides:
        side.wait()
    for half in range(2):

        @pl.loop(0, HALF, step=TILE)
        def _(cols):
            window = pl.ds(pl.multiple_of(cols, TILE), TILE)
            place = pl.ds(pl.multiple_of(half * HALF + cols, TILE), TILE)
            total = base_v[:, place] + left_v[half, :, window].astype(F32) + right_v[half, :, window].astype(F32)
            out_v[:, place] = total.astype(BF16)

        columns = pl.ds(half * HALF, HALF)
        copies.append(pltpu.make_async_copy(out_v.at[:, columns], out.at[0, :, columns], out_sem.at[half]))
        copies[-1].start()
    for copy in copies:
        copy.wait()


def shards(fwd_resid, fwd_query, fwd_keyval, fwd_micro, bwd_query, bwd_keyval, grad_micro, grad_in, out_weight, doc_starts):
    any_space = pl.BlockSpec(memory_space=pl.ANY)
    smem = pl.BlockSpec(memory_space=pltpu.SMEM)
    dma = pltpu.SemaphoreType.DMA
    vmem = pltpu.VMEM
    scratch = [
        pltpu.SMEM((4, 4), jnp.int32),
        vmem((R, R), BF16), vmem((2, R, HD), BF16), vmem((R, R), BF16), vmem((2, R, HD), BF16),
        vmem((R, D), BF16), vmem((R, D), BF16),
        vmem((4, HD, R), BF16), vmem((4, HD, R), BF16), vmem((64, D), BF16),
        vmem((8, 128), jnp.int32), vmem((8, 128), jnp.int32),
        vmem((R, R), F32), vmem((HD, R), BF16), vmem((HD, R), BF16),
        vmem((4, R, R), BF16), vmem((R, R), BF16), vmem((R // 2, R), F32), vmem((R, R), BF16),
        vmem((R, HD), F32), vmem((R, HD), F32), vmem((R, R), BF16), vmem((2, R, HD), BF16), vmem((R, D), BF16),
        vmem((4, 2, 64, D), BF16), vmem((4, 64, D), BF16), vmem((2, 64, HALF), BF16), vmem((2, 64, HALF), BF16),
        vmem((64, HALF), BF16), vmem((64, HALF), BF16),
        vmem((64, HALF), BF16), vmem((64, HALF), BF16), vmem((64, D), F32),
        dma((6,)), dma((4,)), dma((D // TILE,)),
        vmem((CROWS, D), BF16), vmem((CROWS, D), BF16), vmem((CROWS, D), BF16),
        dma, dma, dma, dma, dma((2,)), dma((2,)), dma((3,)), dma((3,)),
        dma((len(PIECES),)), dma((len(PIECES),)), dma, dma, dma((4,)), dma((4,)), dma, dma,
        dma((LAST,)), dma((LAST,)), dma((LAST,)), dma((LAST,)),
        dma((CHUNKS,)), dma((CHUNKS,)), dma((CHUNKS,)), dma((CHUNKS,)),
        dma((4, len(PIECES))), dma((4, len(PIECES))),
        dma((4, 2)), dma((4, 2)), dma((3,)), dma((3,)), dma((3,)), dma((3,)),
    ]
    base, gq, gkv, gw, fin_l, fin_r = pl.pallas_call(
        kernel,
        out_shape=(
            jax.ShapeDtypeStruct((64, D), F32),
            jax.ShapeDtypeStruct((R, R), BF16),
            jax.ShapeDtypeStruct((2, R, HD), BF16),
            jax.ShapeDtypeStruct((R, D), BF16),
            jax.ShapeDtypeStruct((2, 64, HALF), BF16),
            jax.ShapeDtypeStruct((2, 64, HALF), BF16),
        ),
        in_specs=[smem] * 2 + [pl.BlockSpec(memory_space=pltpu.HBM)] * 8,
        out_specs=(any_space,) * 6,
        scratch_shapes=scratch,
        compiler_params=pltpu.CompilerParams(
            collective_id=0, has_side_effects=True, vmem_limit_bytes=40 * 1024 * 1024
        ),
    )(
        fwd_micro, grad_micro, pltpu.with_memory_space_constraint(doc_starts, pltpu.HBM),
        *(
            pltpu.with_memory_space_constraint(a[0], pltpu.HBM)
            for a in (fwd_resid, fwd_query, fwd_keyval, bwd_query, bwd_keyval, grad_in, out_weight)
        ),
    )
    arrays = (gw[None], gq[None], gkv)
    count = R // 64 + 1 + 2
    gw, gq, gkv, out = pl.pallas_call(
        deliver,
        out_shape=(
            *(jax.ShapeDtypeStruct(a.shape, a.dtype) for a in arrays),
            jax.ShapeDtypeStruct((1, 64, D), BF16),
        ),
        in_specs=[any_space] * 6,
        out_specs=(any_space,) * 4,
        scratch_shapes=[
            vmem((64, D), F32), vmem((2, 64, HALF), BF16), vmem((2, 64, HALF), BF16), vmem((64, D), BF16),
            dma((count,)), dma((3,)), dma((2,)),
        ],
        compiler_params=pltpu.CompilerParams(vmem_limit_bytes=8 * 1024 * 1024),
    )(*arrays, base, fin_l, fin_r)
    return (out, gq, gkv[None], gw)


def solution(mesh):
    return jax.shard_map(
        shards,
        mesh=mesh,
        in_specs=(
            P("pipe", "tp", None),
            P("pipe", None, "tp"),
            P("pipe", None, None, "tp"),
            P("pipe"),
            P("pipe", None, "tp"),
            P("pipe", None, None, "tp"),
            P("pipe"),
            P("pipe", "tp", None),
            P("pipe", "tp", None),
            P(),
        ),
        out_specs=(
            P("pipe", "tp", None),
            P("pipe", None, "tp"),
            P("pipe", None, None, "tp"),
            P("pipe", "tp", None),
        ),
        check_vma=False,
    )
```
